32 devices in a mesh: rep: 2 (over x), ea: 16 (over z, y, core).
Axes of the slice: x: 2, y: 2, z: 4, core: 2. Of those that a mesh axis runs over, the one named last changes fastest.
Arguments:
- hidden_in: bfloat16 [512, 4, 4096], P('ea', 'rep'), parts along dimension 1, may hold values from -3 to 3
- queries: bfloat16 [32, 512, 512], P(('rep', 'ea')), parts along dimension 0, may hold values from -112 to 112, as said below
- cache_keys: bfloat16 [32, 512, 128], P(('rep', 'ea')), parts along dimension 0, may hold values from -4 to 4
- cache_values: bfloat16 [32, 512, 128], P(('rep', 'ea')), parts along dimension 0, may hold values from -24 to 24
- new_keys: bfloat16 [32, 512, 128], P(('rep', 'ea')), parts along dimension 0, may hold values from -6 to 6
- new_values: bfloat16 [32, 512, 128], P(('rep', 'ea')), parts along dimension 0, may hold values from -24 to 24
- cache_len: int32 [4], P('rep'), parts along dimension 0, may hold values from 128 to 512, as said below
- out_proj: bfloat16 [4096, 4096], P(None, 'ea'), may hold values from -0.25 to 0.25
- norm_gain: float32 [4096], replicated, may hold values from 0.25 to 1.75
- router: bfloat16 [4096, 16], replicated, may hold values from -0.09375 to 0.09375
- expert_ids: int32 [512, 4, 2], P('ea', 'rep'), parts along dimension 1, may hold values from 0 to 15, all different within a row; in each aligned block of 64 rows (0 to 63, 64 to 127, ..., all dimensions but the last counted through in order) at most 9 rows name the same one
- gate_proj: bfloat16 [4096, 51200], P(None, 'ea'), may hold values from -0.09375 to 0.09375
- up_proj: bfloat16 [4096, 51200], P(None, 'ea'), may hold values from -0.09375 to 0.09375
- down_proj: bfloat16 [51200, 4096], P('ea'), may hold values from -0.109375 to 0.109375
Outputs:
- layer_out: bfloat16 [512, 4, 4096], P('ea', 'rep'), parts along dimension 1
The draws below stay inside these ranges and needn't reach their ends.
There are 2 independent parts, one for each index of `rep`. The reference program is written for one: setup_inputs(seed, part) draws one part's arguments, and reference() takes and returns one part's arrays. A program takes and returns all parts, laid end to end along the dimension named above; an argument that names none is the same for every part. Nothing has to cross between parts.
Inputs may be any that keep to these rules, and one draw needn't show every extreme that they name: `queries`: each entry of the hidden draw may reach the stated range. `cache_len`: some sequence has exactly 512 filled slots. `expert_ids`: the two experts of a row differ. Rows are taken in order of the first two dimensions; in each aligned block of 64 rows (the rows of one device) no expert is named by more than 9 rows, and in some block one expert is named by exactly 9 rows; every expert is named somewhere.
All inputs are finite; a program needn't handle non-finite values.
Results may differ from the reference program's by a relative error of at most 0.0068.
Values may be sent and summed in bfloat16 or wider, within the bound.
A program may use at most 192 MiB of HBM per device.

```python
import math
import jax
import jax.numpy as jnp
import numpy as np
from jax import lax

D = 4096
HQ = 32
KVH = 8
HD = 128
EXPERTS = 16
FFW = 3200
TOPK = 2
CACHE = 512
NEW = 512
SEQS = 2
TOK_DEV = 64
CAP = 9
N_EA = 16


def cache_key_base(key):
    base = jax.random.normal(jax.random.fold_in(key, 7), (SEQS * KVH, CACHE, HD), jnp.float32)
    return jnp.clip(base, -4.0, 4.0)


def draw_cache_keys(key, part):
    base = cache_key_base(key)
    return base.astype(jnp.bfloat16)


def draw_queries(key, part):
    base = jax.random.normal(jax.random.fold_in(key, 11), (SEQS * KVH, NEW, HQ // KVH * HD), jnp.float32)
    base = jnp.clip(base, -4.5, 4.5)
    return base.astype(jnp.bfloat16)


def draw_cache_len(key, part):
    filled = jax.random.randint(jax.random.fold_in(key, 3), (SEQS,), CACHE // 4, CACHE + 1)
    longest = jax.random.randint(jax.random.fold_in(key, 5), (), 0, SEQS)
    return filled.at[longest].set(CACHE).astype(jnp.int32)


def shard_levels(stream_key, dims, split, smallest, largest):
    gain, own = 1.0, jax.random.fold_in(stream_key, 6)
    for axis_at, shards_of in split:
        heights = jnp.exp(jax.random.uniform(jax.random.fold_in(own, axis_at), (shards_of,), jnp.float32, smallest / len(split), largest / len(split)))
        gain = gain * jnp.repeat(heights, dims[axis_at] // shards_of).reshape([-1 if axis == axis_at else 1 for axis in range(len(dims))])
    return gain


def deal_out(rng, own, number, rows, amount, top, most, slope):
    order = jax.random.permutation(rng, amount)
    packed, ordinary = portions_of(amount, rows * top, most, slope, True), portions_of(amount, rows * top, most, slope, False)
    places = jnp.arange(amount)

    def named(tallies, turn):
        used = int((tallies > 0).sum())
        fixed = max(1, used // 4)
        moved = fixed + (places - fixed + turn * (used - fixed)) % max(1, amount - fixed)
        return jnp.zeros((amount,), jnp.int32).at[order[jnp.where(places < fixed, places, moved)]].set(jnp.asarray(tallies, jnp.int32))

    tallies = jnp.where(number % 4 == 0, named(packed, number // 4), named(ordinary, number - number // 4 - 1))
    mixed = jax.random.permutation(jax.random.fold_in(own, 3), amount)
    giver, sink = mixed[0:amount // 2 * 2:2], mixed[1:amount // 2 * 2:2]
    margin = jnp.minimum(tallies[giver] - 1, most - tallies[sink]) // 2
    margin = jnp.where((giver == order[0]) | (sink == order[0]) | (tallies[sink] == 0), 0, jnp.maximum(margin, 0))
    moved = jax.random.randint(jax.random.fold_in(own, 4), (amount // 2,), 0, 1 << 20) % (margin + 1)
    tallies = tallies.at[giver].add(-moved).at[sink].add(moved)
    labels = jnp.searchsorted(jnp.cumsum(tallies), jnp.arange(rows * top), side="right").astype(jnp.int32)
    listing = labels.reshape(top, rows).T
    listing = listing[jax.random.permutation(jax.random.fold_in(own, 1), rows)]
    turn = jax.random.randint(jax.random.fold_in(own, 2), (rows, 1), 0, top)
    return jnp.take_along_axis(listing, (jnp.arange(top)[None, :] + turn) % top, axis=1)


def portions_of(amount, total, limit, lean, full):
    weights = [(1 << 20) // math.isqrt(standing ** lean) + 1 for standing in range(1, amount + 1)]
    largest = limit if full else min(limit, max(-(-total // amount), total * weights[0] // sum(weights)))
    least = 1 if total - largest >= amount - 1 else 0
    holding, rest = [largest] + [least] * (amount - 1), total - largest - least * (amount - 1)
    while rest > 0:
        candidates = [i for i in range(1, amount) if holding[i] < largest] or [i for i in range(1, amount) if holding[i] < limit]
        mass, remaining = sum([weights[i] for i in candidates]), rest
        for i in candidates:
            extra = min(limit - holding[i], max(1, remaining * weights[i] // mass), rest)
            holding[i] = holding[i] + extra
            rest = rest - extra
    return np.array(holding)


def centred(rng, dims, scale, bound, split=(), kind=jnp.bfloat16):
    entries = jax.random.normal(rng, dims, jnp.float32) * scale
    if len(split) > 0:
        entries = shard_levels(rng, dims, split, -0.22, 0.18) * entries
    return jnp.clip(entries, min=-bound, max=bound).astype(kind)


def setup_inputs(seed: int = 0, part: int = 0) -> dict:
    keys = jax.random.split(jax.random.key(seed), 15)
    part_keys = jax.random.split(jax.random.fold_in(keys[14], part), 15)
    hidden_in = centred(part_keys[0], (NEW, SEQS, D), 0.5, 3.0, ((0, 16),))
    queries = draw_queries(jax.random.fold_in(jax.random.fold_in(keys[14], part), 71), part)
    cache_keys = draw_cache_keys(jax.random.fold_in(jax.random.fold_in(keys[14], part), 71), part)
    cache_values = centred(part_keys[3], (SEQS * KVH, CACHE, HD), 4.0, 24.0, ((0, 16),))
    new_keys = centred(part_keys[4], (SEQS * KVH, NEW, HD), 1.0, 6.0, ((0, 16),))
    new_values = centred(part_keys[5], (SEQS * KVH, NEW, HD), 4.0, 24.0, ((0, 16),))
    cache_len = draw_cache_len(jax.random.fold_in(jax.random.fold_in(keys[14], part), 71), part)
    out_proj = centred(keys[7], (HQ * HD, D), (HQ * HD // 8) ** -0.5, 0.25, ((1, 16),))
    norm_gain = jnp.clip(1.0 + 0.15 * jax.random.normal(keys[8], (D,), jnp.float32), 0.25, 1.75)
    router = centred(keys[9], (D, EXPERTS), D ** -0.5, 0.09375)
    expert_ids_keys = jax.random.split(jax.random.fold_in(part_keys[10], 1), NEW * SEQS // TOK_DEV)
    expert_ids_turns = jax.random.permutation(jax.random.fold_in(part_keys[10], 3), NEW * SEQS // TOK_DEV)
    expert_ids = jax.vmap(lambda own, number: deal_out(jax.random.fold_in(part_keys[10], 2), own, number, TOK_DEV, EXPERTS, TOPK, CAP, 2))(expert_ids_keys, expert_ids_turns).reshape((NEW, SEQS, TOPK))
    gate_proj = centred(keys[11], (D, EXPERTS * FFW), D ** -0.5, 0.09375, ((1, 16),))
    up_proj = centred(keys[12], (D, EXPERTS * FFW), D ** -0.5, 0.09375, ((1, 16),))
    down_proj = centred(keys[13], (EXPERTS * FFW, D), FFW ** -0.5, 0.109375, ((0, 16),))
    return {"hidden_in": hidden_in, "queries": queries, "cache_keys": cache_keys, "cache_values": cache_values, "new_keys": new_keys, "new_values": new_values, "cache_len": cache_len, "out_proj": out_proj, "norm_gain": norm_gain, "router": router, "expert_ids": expert_ids, "gate_proj": gate_proj, "up_proj": up_proj, "down_proj": down_proj}


def reference(hidden_in, queries, cache_keys, cache_values, new_keys, new_values, cache_len, out_proj, norm_gain, router, expert_ids, gate_proj, up_proj, down_proj):
    group_q = HQ // KVH
    seq_count = N_EA // KVH
    shard_count = N_EA // EXPERTS
    hid_width = FFW // shard_count
    score_scale = 1.0 / math.sqrt(HD)
    position = jnp.arange(NEW, dtype=jnp.int32)
    key_pos = jnp.arange(CACHE + NEW, dtype=jnp.int32)

    def attend(attn_unit):
        query_rows = queries[attn_unit].reshape(NEW, group_q, HD).astype(jnp.float32)
        all_keys = jnp.concatenate([cache_keys[attn_unit], new_keys[attn_unit]], axis=0).astype(jnp.float32)
        all_values = jnp.concatenate([cache_values[attn_unit], new_values[attn_unit]], axis=0).astype(jnp.float32)
        visible = cache_len[attn_unit // KVH]
        allowed = jnp.where(key_pos[None, :] < CACHE, key_pos[None, :] < visible, key_pos[None, :] - CACHE <= position[:, None])
        scores = jnp.einsum('qhd,kd->hqk', query_rows, all_keys) * score_scale
        scores = jnp.where(allowed[None], scores, jnp.float32(-1e+30))
        top_score = lax.optimization_barrier(jnp.max(scores, axis=2, keepdims=True))
        exp_scores = jnp.exp(scores - top_score)
        attn_probs = lax.optimization_barrier((exp_scores / lax.optimization_barrier(jnp.sum(exp_scores, axis=2, keepdims=True))).astype(jnp.bfloat16))
        attended = jnp.einsum('hqk,kd->qhd', attn_probs.astype(jnp.float32), all_values).astype(jnp.bfloat16).reshape(NEW, group_q * HD)
        group_proj = lax.dynamic_slice_in_dim(out_proj, attn_unit % KVH * group_q * HD, group_q * HD, 0)
        return jnp.dot(attended, group_proj, preferred_element_type=jnp.float32).astype(jnp.bfloat16)
    head_terms = lax.optimization_barrier(lax.map(attend, jnp.arange(N_EA, dtype=jnp.int32)))
    head_sum = lax.optimization_barrier(jnp.sum(head_terms.reshape(seq_count, KVH, NEW, D).astype(jnp.float32), axis=1))
    residual = hidden_in.astype(jnp.float32) + jnp.transpose(head_sum, (1, 0, 2))
    flat_res = residual.reshape(NEW * seq_count, D)
    mean_sq = lax.optimization_barrier(jnp.mean(flat_res * flat_res, axis=1, keepdims=True))
    normed = (flat_res * lax.rsqrt(mean_sq + 1e-05) * norm_gain[None, :]).astype(jnp.bfloat16)
    logits = jnp.dot(normed, router, preferred_element_type=jnp.float32)
    route_ids = expert_ids.reshape(NEW * seq_count, TOPK)
    chosen = jnp.take_along_axis(logits, route_ids, axis=1)
    first_gate = jax.nn.sigmoid(chosen[:, 0:1] - chosen[:, 1:2])
    flat_ids = route_ids.reshape(-1)
    capacity = N_EA * CAP
    one_hot = (flat_ids[:, None] == jnp.arange(EXPERTS, dtype=jnp.int32)[None, :]).astype(jnp.int32)
    slot_rank = lax.optimization_barrier(jnp.sum((jnp.cumsum(one_hot, axis=0) - one_hot) * one_hot, axis=1)).astype(jnp.int32)

    def run_expert(expert):
        members = jnp.argsort((flat_ids != expert).astype(jnp.int32), stable=True)[:capacity]
        routed_rows = normed[members // TOPK]
        gate_cols = lax.dynamic_slice_in_dim(gate_proj, expert * FFW, FFW, 1)
        up_cols = lax.dynamic_slice_in_dim(up_proj, expert * FFW, FFW, 1)
        gate_val = jnp.dot(routed_rows, gate_cols, preferred_element_type=jnp.float32)
        up_val = jnp.dot(routed_rows, up_cols, preferred_element_type=jnp.float32)
        inner_act = (jax.nn.silu(gate_val) * up_val).astype(jnp.bfloat16)
        shard_total = jnp.zeros((capacity, D), jnp.float32)
        for shard_num in range(shard_count):
            down_rows = lax.dynamic_slice_in_dim(down_proj, expert * FFW + shard_num * hid_width, hid_width, 0)
            shard_term = jnp.dot(inner_act[:, shard_num * hid_width:(shard_num + 1) * hid_width], down_rows, preferred_element_type=jnp.float32).astype(jnp.bfloat16)
            shard_total = shard_total + lax.optimization_barrier(shard_term).astype(jnp.float32)
        return shard_total
    expert_out = lax.map(run_expert, jnp.arange(EXPERTS, dtype=jnp.int32))
    picked = expert_out[flat_ids, slot_rank].reshape(NEW * seq_count, TOPK, D)
    mixed = flat_res + first_gate * picked[:, 0] + (1.0 - first_gate) * picked[:, 1]
    return mixed.astype(jnp.bfloat16).reshape(NEW, seq_count, D)
```

```python
import functools
import math

import jax
import jax.numpy as jnp
from jax import lax
from jax.experimental import pallas as pl
from jax.experimental.pallas import tpu as pltpu
from jax.sharding import PartitionSpec as P

HQ = 32
KVH = 8
HD = 128
EXPERTS = 16
TOPK = 2
CAP = 9


def expert_terms(received, gate_proj, up_proj, down_proj):
    src_count, slot_count, model_width = received.shape
    flat_rows = received.reshape(src_count * slot_count, model_width)
    gate_val = jnp.dot(flat_rows, gate_proj, preferred_element_type=jnp.float32)
    up_val = jnp.dot(flat_rows, up_proj, preferred_element_type=jnp.float32)
    inner_act = (jax.nn.silu(gate_val) * up_val).astype(jnp.bfloat16)
    shard_term = jnp.dot(inner_act, down_proj, preferred_element_type=jnp.float32).astype(
        jnp.bfloat16
    )
    return shard_term.reshape(src_count, slot_count, model_width)


def expert_half(received, gate_proj, up_proj, down_proj):
    shard_term = expert_terms(received, gate_proj, up_proj, down_proj)
    return lax.all_to_all(shard_term, "ea", split_axis=0, concat_axis=0, tiled=True)


def route_rows(normed, route_ids, first_gate, gate_proj, up_proj, down_proj):
    row_count, model_width = normed.shape
    dev_count = lax.axis_size("ea")
    shard_count = dev_count // EXPERTS
    flat_ids = route_ids.reshape(-1)
    pair_count = flat_ids.shape[0]
    expert_cols = jnp.arange(EXPERTS, dtype=jnp.int32)
    one_hot = (flat_ids[:, None] == expert_cols[None, :]).astype(jnp.float32)
    pair_order = jnp.arange(pair_count, dtype=jnp.int32)
    earlier = (pair_order[:, None] > pair_order[None, :]).astype(jnp.float32)
    before = jnp.dot(earlier, one_hot, precision=lax.Precision.HIGHEST)
    slot_pos = jnp.sum(before * one_hot, axis=1).astype(jnp.int32)
    target = (flat_ids * CAP + slot_pos).reshape(row_count, TOPK)
    slot_ids = jnp.arange(EXPERTS * CAP, dtype=jnp.int32)
    select = (
        (target[None, :, 0] == slot_ids[:, None]) | (target[None, :, 1] == slot_ids[:, None])
    ).astype(jnp.bfloat16)
    packed = jnp.dot(select, normed, preferred_element_type=jnp.float32).astype(jnp.bfloat16)
    packed = jnp.broadcast_to(
        packed.reshape(EXPERTS, 1, CAP, model_width), (EXPERTS, shard_count, CAP, model_width)
    )
    packed = packed.reshape(dev_count, CAP, model_width)
    first_slots = (CAP + 1) // 2
    bounds = [(0, first_slots), (first_slots, CAP)]
    pieces = []
    for lower, upper in bounds:
        part_block = packed[:, lower:upper]
        pieces.append(
            (lambda received: expert_half(received, gate_proj, up_proj, down_proj))(
                lax.all_to_all(part_block, "ea", split_axis=0, concat_axis=0, tiled=True)
            )
        )
    returned = jnp.concatenate(pieces, axis=1)
    expert_out = jnp.sum(
        returned.reshape(EXPERTS, shard_count, CAP, model_width).astype(jnp.float32), axis=1
    )
    expert_out = expert_out.reshape(EXPERTS * CAP, model_width)
    picked = jnp.take(expert_out, target, axis=0)
    return first_gate * picked[:, 0] + (1.0 - first_gate) * picked[:, 1]


def wide_body(
    hidden_in,
    queries,
    cache_keys,
    cache_values,
    new_keys,
    new_values,
    cache_len,
    out_proj,
    norm_gain,
    router,
    expert_ids,
    gate_proj,
    up_proj,
    down_proj,
):
    dev_count = lax.axis_size("ea")
    dev_index = lax.axis_index("ea")
    new_rows = queries.shape[1]
    group_q = HQ // KVH
    seq_count = dev_count // KVH
    piece_rows = new_rows // dev_count
    cache_rows = cache_keys.shape[1]
    col_width = out_proj.shape[1]
    model_width = hidden_in.shape[2]
    score_scale = 1.0 / math.sqrt(HD)
    visible = lax.dynamic_index_in_dim(cache_len, dev_index // KVH, keepdims=False)
    position = (
        jnp.arange(new_rows, dtype=jnp.int32).reshape(dev_count, piece_rows).T.reshape(new_rows)
    )
    query_rows = (
        queries[0]
        .reshape(dev_count, piece_rows, group_q, HD)
        .transpose(1, 0, 2, 3)
        .reshape(new_rows, group_q, HD)
    )
    all_keys = jnp.concatenate([cache_keys[0], new_keys[0]], axis=0)
    all_values = jnp.concatenate([cache_values[0], new_values[0]], axis=0)
    key_pos = jnp.arange(cache_rows + new_rows, dtype=jnp.int32)
    allowed = jnp.where(
        key_pos[None, :] < cache_rows,
        key_pos[None, :] < visible,
        key_pos[None, :] - cache_rows <= position[:, None],
    )
    scores = (
        jnp.einsum("qhd,kd->hqk", query_rows, all_keys, preferred_element_type=jnp.float32)
        * score_scale
    )
    scores = jnp.where(allowed[None], scores, jnp.float32(-1e30))
    top_score = jnp.max(scores, axis=2, keepdims=True)
    exp_scores = jnp.exp(scores - top_score)
    attn_probs = (exp_scores / jnp.sum(exp_scores, axis=2, keepdims=True)).astype(jnp.bfloat16)
    attended = jnp.einsum("hqk,kd->qhd", attn_probs, all_values, preferred_element_type=jnp.float32)
    attended = attended.astype(jnp.bfloat16).reshape(new_rows, group_q * HD)
    local_rows = out_proj.reshape(KVH, group_q * HD, col_width).transpose(1, 0, 2)
    outgoing = jnp.broadcast_to(local_rows[:, None], (group_q * HD, seq_count, KVH, col_width))
    outgoing = outgoing.reshape(group_q * HD, dev_count, col_width)
    group_proj = lax.all_to_all(outgoing, "ea", split_axis=1, concat_axis=1, tiled=True).reshape(
        group_q * HD, model_width
    )
    head_part = jnp.dot(attended, group_proj, preferred_element_type=jnp.float32).astype(
        jnp.bfloat16
    )
    arrived = lax.all_to_all(
        head_part.reshape(piece_rows, dev_count, model_width),
        "ea",
        split_axis=1,
        concat_axis=1,
        tiled=True,
    )
    head_sum = jnp.sum(
        arrived.reshape(piece_rows, seq_count, KVH, model_width).astype(jnp.float32), axis=2
    )
    residual = hidden_in.astype(jnp.float32) + head_sum
    flat_res = residual.reshape(piece_rows * seq_count, model_width)
    mean_sq = jnp.mean(flat_res * flat_res, axis=1, keepdims=True)
    normed = (flat_res * lax.rsqrt(mean_sq + 1e-05) * norm_gain[None, :]).astype(jnp.bfloat16)
    logits = jnp.dot(normed, router, preferred_element_type=jnp.float32)
    route_ids = expert_ids.reshape(piece_rows * seq_count, TOPK)
    chosen = jnp.take_along_axis(logits, route_ids, axis=1)
    first_gate = jax.nn.sigmoid(chosen[:, 0:1] - chosen[:, 1:2])
    expert_mix = route_rows(normed, route_ids, first_gate, gate_proj, up_proj, down_proj)
    result_rows = (flat_res + expert_mix).astype(jnp.bfloat16)
    return result_rows.reshape(piece_rows, seq_count, model_width)


NZ = 4
NDEV = 16
MAIN = 8
SLOTS = EXPERTS * CAP
F32 = jnp.float32
BF16 = jnp.bfloat16


def attend(q, ck, cv, nk, nv, visible, first_row):
    contract = (((1,), (1,)), ((), ()))
    rows, cached, fresh = q.shape[0], ck.shape[0], nk.shape[0]
    scale = 1.0 / math.sqrt(HD)
    old = lax.dot_general(q, ck, contract, preferred_element_type=F32) * scale
    new = lax.dot_general(q, nk, contract, preferred_element_type=F32) * scale
    old_pos = lax.broadcasted_iota(jnp.int32, (rows, cached), 1)
    row_pos = lax.broadcasted_iota(jnp.int32, (rows, fresh), 0) + first_row
    new_pos = lax.broadcasted_iota(jnp.int32, (rows, fresh), 1)
    old = jnp.where(old_pos < visible, old, -1e30)
    new = jnp.where(new_pos <= row_pos, new, -1e30)
    top = jnp.maximum(
        jnp.max(old, axis=1, keepdims=True), jnp.max(new, axis=1, keepdims=True)
    )
    old = jnp.exp(old - top)
    new = jnp.exp(new - top)
    total = jnp.sum(old, axis=1, keepdims=True) + jnp.sum(new, axis=1, keepdims=True)
    mixed = jnp.dot(old.astype(BF16), cv, preferred_element_type=F32)
    mixed += jnp.dot(new.astype(BF16), nv, preferred_element_type=F32)
    return (mixed / total).astype(BF16)


def remote(src, dst, send, recv, dev):
    return pltpu.make_async_remote_copy(
        src_ref=src,
        dst_ref=dst,
        send_sem=send,
        recv_sem=recv,
        device_id={"ea": dev},
        device_id_type=pl.DeviceIdType.MESH,
    )


def greet(me):
    barrier = pltpu.get_barrier_semaphore()

    def hello(off, carry):
        pl.semaphore_signal(
            barrier,
            inc=1,
            device_id={"ea": lax.rem(me + off, NDEV)},
            device_id_type=pl.DeviceIdType.MESH,
        )
        return carry

    lax.fori_loop(1, NDEV, hello, 0)


def greeted():
    pl.semaphore_wait(pltpu.get_barrier_semaphore(), NDEV - 1)


def others(me, step):
    def go(off, carry):
        step(lax.rem(me + off, NDEV))
        return carry

    lax.fori_loop(1, NDEV, go, 0)


TILE = 640
TILES = 5
GU_SLOTS = 3
DN_SLOTS = 2
ROW_CUTS = 2
HEAD_CUTS = 2
PIECES = ROW_CUTS * HEAD_CUTS
BLOCKS = NDEV // ROW_CUTS
PART_SLOTS = BLOCKS * CAP
BACK = 1024


def layer_kernel(
    len_ref, q_hbm, ck_hbm, cv_hbm, nk_hbm, nv_hbm, proj_hbm, hid_hbm, gain_ref, router_hbm, ids_ref, gate_hbm, up_hbm, down_hbm,
    out_ref,
    q_ref, ck_ref, cv_ref, nk_ref, nv_ref,
    buf, acc, hid_got, ids_got, proj_ref, router_ref, resid, code_ref, name_ref, sel_ref, info_ref, place_ref,
    out_go, out_got, raw_ref, xg_ref, ss_ref, lg_ref, gacc, uacc, inner, back_go, back_got, fold_back, back_raw, terms, gu, dn,
    in_sem, gu_sem, dn_sem,
    block_sem, left_sem, right_sem, y_sem, core_sem,
    hid_send, hid_recv, ids_send, ids_recv, go_send, go_recv, back_send, back_recv,
):
    me = lax.axis_index("ea")
    model = gain_ref.shape[1]
    width = proj_ref.shape[1]
    mine = hid_got.shape[1]
    piece = mine // 2
    tall, part = buf.shape[2], buf.shape[3]
    span = resid.shape[0]
    wide = gu.shape[2]
    z, y, c = me // 4, (me // 2) % 2, me % 2

    def index(zz, yy, cc):
        return (zz * 2 + yy) * 2 + cc

    def fetch(src, dst, slot):
        return pltpu.make_async_copy(src, dst, in_sem.at[slot])

    col_me = pl.ds(pl.multiple_of(me * width, width), width)
    loads = [
        (q_hbm, q_ref), (ck_hbm, ck_ref), (nk_hbm, nk_ref), (cv_hbm, cv_ref), (nv_hbm, nv_ref),
        (proj_hbm, proj_ref), (hid_hbm.at[:, col_me], hid_got.at[me]), (router_hbm, router_ref),
    ]
    for slot, load in enumerate(loads):
        fetch(*load, slot).start()
    greet(me)

    def chip_at(s):
        low = (z + s // 2) % 2
        high = (z // 2 + s // 4) % 2
        return (high * 2 + low) * 2 + (y + s) % 2

    def gate_up(s):
        rows = pl.ds(pl.multiple_of(chip_at(s) * wide, wide), wide)
        slot = s % GU_SLOTS
        return [
            pltpu.make_async_copy(src.at[rows, :], gu.at[slot, n], gu_sem.at[slot, n])
            for n, src in enumerate((gate_hbm, up_hbm))
        ]

    def down(n):
        cols = pl.ds(pl.multiple_of(n * BACK, BACK), BACK)
        slot = n % DN_SLOTS
        return pltpu.make_async_copy(down_hbm.at[:, cols], dn.at[slot], dn_sem.at[slot])

    for s in range(GU_SLOTS):
        for copy in gate_up(s):
            copy.start()
    for n in range(DN_SLOTS):
        down(n).start()

    def hid_copy(dev):
        cols = pl.ds(pl.multiple_of(dev * width, width), width)
        return remote(
            hid_hbm.at[:, cols], hid_got.at[me], hid_send.at[dev], hid_recv.at[me], dev
        )

    def hid_landed(dev):
        remote(
            hid_hbm.at[:, col_me], hid_got.at[dev], hid_send.at[dev], hid_recv.at[dev], dev
        ).wait_recv()

    def ids_copy(src, dev):
        return remote(
            ids_got.at[src], ids_got.at[src], ids_send.at[dev], ids_recv.at[src], dev
        )

    def block_copy(p, blk, sem, dev):
        return remote(buf.at[p, blk], buf.at[p, blk], sem, block_sem.at[p, blk], dev)

    def to_left(p, zz):
        return block_copy(p, index(zz, y, c), left_sem.at[p, zz], index(z - 1, y, c))

    def to_right(p, zz):
        return block_copy(p, index(zz, y, c), right_sem.at[p, zz], index(z + 1, y, c))

    def to_y(p, zz):
        return block_copy(p, index(zz, y, c), y_sem.at[p, zz], index(z, 1 - y, c))

    def to_core(p, zz, yy):
        return block_copy(p, index(zz, yy, c), core_sem.at[p, zz * 2 + yy], index(z, y, 1 - c))

    def landed(p, blk):
        block_copy(p, blk, left_sem.at[p, 0], index(z, y, 1 - c)).wait_recv()

    def line(p, zz, go_left, go_right):
        if go_left:
            @pl.when(z > 0)
            def _():
                to_left(p, zz).start()
        if go_right:
            @pl.when(z < NZ - 1)
            def _():
                to_right(p, zz).start()
        to_y(p, zz).start()
        to_core(p, zz, y).start()

    def pair(d, step):
        @pl.when(z + d < NZ)
        def _():
            step(z + d, True)

        @pl.when(z - d >= 0)
        def _():
            step(z - d, False)

    def arrive_line(p, d):
        def step(zz, from_right):
            landed(p, index(zz, y, c))
            line(p, zz, from_right, not from_right)

        pair(d, step)

    def across(p, zz):
        landed(p, index(zz, 1 - y, c))
        to_core(p, zz, 1 - y).start()

    def arrive_y(p, d):
        if d == 0:
            across(p, z)
        else:
            pair(d, lambda zz, _: across(p, zz))

    def multiply(r, d):
        def go(n, carry):
            side, yy, cc = n % 2, (n // 2) % 2, n // 4
            zz = z + d * (1 - 2 * side)
            ok = (zz >= 0) & (zz < NZ)
            if d == 0:
                ok = ok & (side == 0)

            @pl.when(ok)
            def _():
                blk = index(zz, (y + yy) % 2, (c + cc) % 2)

                @pl.when(cc == 1)
                def _():
                    for h in range(HEAD_CUTS):
                        landed(r * HEAD_CUTS + h, blk)

                group = blk % KVH
                total = acc[r, blk // KVH]
                for h in range(HEAD_CUTS):
                    start = (group * HEAD_CUTS + h) * part
                    rows = pl.ds(pl.multiple_of(start, part), part)
                    total += jnp.dot(
                        buf[r * HEAD_CUTS + h, blk], proj_ref[rows, :], preferred_element_type=F32
                    )
                acc[r, blk // KVH] = total

            return carry

        lax.fori_loop(0, 8, go, 0)

    for slot in range(5):
        fetch(*loads[slot], slot).wait()
    visible = len_ref[me // KVH]

    def attention(r, h):
        keys = slice(0, (r + 1) * tall)

        def head(n, carry):
            src = pl.ds(pl.multiple_of(h * part + n * HD, HD), HD)
            dst = pl.ds(pl.multiple_of(n * HD, HD), HD)
            buf[r * HEAD_CUTS + h, me, :, dst] = attend(
                q_ref[r * tall : (r + 1) * tall, src], ck_ref[...], cv_ref[...],
                nk_ref[keys], nv_ref[keys], visible, r * tall,
            )
            return carry

        lax.fori_loop(0, part // HD, head, 0)

    ids_got[me] = jnp.concatenate([ids_ref[0], ids_ref[1]], axis=1)
    attention(0, 0)
    greeted()
    line(0, z, True, True)
    others(me, lambda dev: ids_copy(me, dev).start())
    others(me, lambda dev: hid_copy(dev).start())
    for r in range(ROW_CUTS):
        for h in range(HEAD_CUTS):
            if r or h:
                attention(r, h)
                line(r * HEAD_CUTS + h, z, True, True)
    acc[...] = jnp.zeros_like(acc)
    gacc[...] = jnp.zeros_like(gacc)
    uacc[...] = jnp.zeros_like(uacc)
    ss_ref[...] = jnp.zeros_like(ss_ref)
    lg_ref[...] = jnp.zeros_like(lg_ref)
    fetch(*loads[5], 5).wait()

    def ranks(ids, block):
        lanes = ids.shape[1]
        rows = lax.broadcasted_iota(jnp.int32, (EXPERTS, lanes), 0)
        first = (ids[0:1] == rows).astype(F32)
        second = (ids[1:2] == rows).astype(F32)
        one = lax.broadcasted_iota(jnp.int32, (lanes, lanes), 0)
        two = lax.broadcasted_iota(jnp.int32, (lanes, lanes), 1)
        same = (one // block) == (two // block)
        tri = ((one < two) & same).astype(F32)
        before0 = jnp.dot(first, tri, preferred_element_type=F32)
        before1 = jnp.dot(second, tri, preferred_element_type=F32) + jnp.dot(
            first, same.astype(F32), preferred_element_type=F32
        )
        return (
            jnp.sum(before0 * first, axis=0, keepdims=True),
            jnp.sum(before1 * second, axis=0, keepdims=True),
        )

    def own_places():
        ids = ids_got[me]
        spots = lax.broadcasted_iota(jnp.int32, (SLOTS, mine), 0).astype(F32)
        total = jnp.zeros((SLOTS, mine), F32)
        for k, rank in enumerate(ranks(ids, mine)):
            expert = ids[k : k + 1].astype(F32)
            where = jnp.where(rank < MAIN - 0.5, expert * MAIN + rank, EXPERTS * MAIN + expert)
            total += (spots == where).astype(F32)
        place_ref[...] = total.T.astype(BF16)

    def codes():
        others(me, lambda dev: ids_copy(dev, dev).wait_recv())
        for q in range(NDEV // 2):
            ids = jnp.concatenate([ids_got[2 * q], ids_got[2 * q + 1]], axis=1)
            r, at = 2 * q // BLOCKS, (2 * q % BLOCKS) * mine
            lane = lax.broadcasted_iota(jnp.int32, (1, 2 * mine), 1)
            block = ((at + lane) // mine).astype(F32)
            cols = slice(at, at + 2 * mine)
            for k, rank in enumerate(ranks(ids, mine)):
                name = ids[k : k + 1].astype(F32)
                spot = jnp.where(rank < MAIN - 0.5, block * MAIN + rank, BLOCKS * MAIN + block)
                code_ref[r, k : k + 1, cols] = name * PART_SLOTS + spot
                name_ref[r, k : k + 1, cols] = name

    def spots_of(e):
        rows = lax.broadcasted_iota(jnp.int32, (PART_SLOTS, span), 0)
        return (rows + e * PART_SLOTS).astype(F32)

    def selects(r):
        def go(e, carry):
            spots = spots_of(e)
            hit = (spots == code_ref[r, 0:1, :]) | (spots == code_ref[r, 1:2, :])
            sel_ref[r, e] = hit.astype(F32).astype(BF16)
            return carry

        lax.fori_loop(0, EXPERTS, go, 0)

    def infos():
        for r in range(ROW_CUTS):
            spots = spots_of(me)
            hit0 = (spots == code_ref[r, 0:1, :]).astype(F32)
            hit1 = (spots == code_ref[r, 1:2, :]).astype(F32)
            chosen = jnp.sum(hit0, axis=1, keepdims=True)
            other = jnp.sum(
                hit0 * name_ref[r, 1:2, :] + hit1 * name_ref[r, 0:1, :], axis=1, keepdims=True
            )
            rows = slice(r * PART_SLOTS, (r + 1) * PART_SLOTS)
            info_ref[0, rows, :] = jnp.broadcast_to(chosen, (PART_SLOTS, info_ref.shape[2]))
            info_ref[1, rows, :] = jnp.broadcast_to(other, (PART_SLOTS, info_ref.shape[2]))

    def go_copy(r, src, dev):
        return remote(
            out_go.at[r, dev], out_got.at[r, src], go_send.at[r, dev], go_recv.at[r, src], dev
        )

    def dispatch(r):
        for b in range(BLOCKS):
            for s in range(2):
                rows = slice(b * piece, (b + 1) * piece)
                at = b * mine + s * piece
                value = acc[r, s, rows, :] + hid_got[
                    r * BLOCKS + b, s * piece : (s + 1) * piece, :
                ].astype(F32)
                resid[at : at + piece, :] = value.astype(BF16)

        def send(i, carry):
            dev = (me + 7 * i) % NDEV
            out_go[r, dev] = jnp.dot(
                sel_ref[r, dev], resid[...], preferred_element_type=F32
            ).astype(BF16)
            go_copy(r, me, dev).start()
            return carry

        lax.fori_loop(1, NDEV, send, 0)
        out_got[r, me] = jnp.dot(
            sel_ref[r, me], resid[...], preferred_element_type=F32
        ).astype(BF16)

    def arrive(r, d):
        for h in range(HEAD_CUTS):
            p = r * HEAD_CUTS + h
            if d < NZ:
                arrive_line(p, d)
            arrive_y(p, d - 1)

    plan = [(0, 1), (0, 2), (1, 1), (0, 3), (1, 2), (0, 4), (1, 3), (1, 4)]
    for n, (r, d) in enumerate(plan):
        arrive(r, d)
        if n == 0:
            own_places()
            codes()
        if n == 1:
            selects(0)
        if n == 2:
            selects(1)
            infos()
        multiply(r, d - 1)
        if d == NZ:
            if r == 0:
                others(me, hid_landed)
                fetch(*loads[6], 6).wait()
            dispatch(r)
    fetch(*loads[7], 7).wait()

    def gather(ref, dev, at):
        for r in range(ROW_CUTS):
            rows = slice(r * PART_SLOTS, (r + 1) * PART_SLOTS)
            ref[rows, at : at + width] = out_got[r, dev].astype(F32)

    steps = model // wide

    def take(s):
        chip = chip_at(s)
        for n in range(2):
            dev = chip * 2 + n

            @pl.when(dev != me)
            def _():
                for r in range(ROW_CUTS):
                    go_copy(r, dev, dev).wait_recv()

            gather(raw_ref, dev, n * width)
        raw = raw_ref[...]
        cols = pl.ds(pl.multiple_of(chip * wide, wide), wide)
        xg_ref[...] = (raw * gain_ref[:, cols]).astype(BF16)
        ss_ref[...] += jnp.broadcast_to(jnp.sum(raw * raw, axis=1, keepdims=True), ss_ref.shape)
        lg_ref[...] += lax.dot_general(
            xg_ref[...], router_ref[:, cols], (((1,), (1,)), ((), ())), preferred_element_type=F32
        )
        for copy in gate_up(s):
            copy.wait()

    def products(s, t):
        cols = pl.ds(pl.multiple_of(t * TILE, TILE), TILE)
        slot = s % GU_SLOTS
        gate = gacc[t] + jnp.dot(xg_ref[...], gu[slot, 0, :, cols], preferred_element_type=F32)
        up = uacc[t] + jnp.dot(xg_ref[...], gu[slot, 1, :, cols], preferred_element_type=F32)
        return gate, up

    def expert_step(s, carry):
        take(s)

        def tile_step(t, carry):
            gate, up = products(s, t)
            gacc[t] = gate
            uacc[t] = up
            return carry

        lax.fori_loop(0, TILES, tile_step, 0)

        @pl.when(s + GU_SLOTS < steps)
        def _():
            for copy in gate_up(s + GU_SLOTS):
                copy.start()

        return carry

    lax.fori_loop(0, steps - 1, expert_step, 0)
    take(steps - 1)
    scale = lax.rsqrt(ss_ref[:, 0:1] / model + 1e-05)
    names = lax.broadcasted_iota(jnp.int32, lg_ref.shape, 1).astype(F32)
    mine_at = (names == me.astype(F32)).astype(F32)
    other_at = (names == info_ref[1, :, 0:1]).astype(F32)
    gap = jnp.sum(lg_ref[...] * (mine_at - other_at), axis=1, keepdims=True) * scale
    info_ref[1] = jnp.broadcast_to(jax.nn.sigmoid(gap), info_ref.shape[1:])

    def last_step(t, carry):
        gate, up = products(steps - 1, t)
        gate, up = gate * scale, up * scale
        cols = pl.ds(pl.multiple_of(t * TILE, TILE), TILE)
        inner[:, cols] = (gate / (1.0 + jnp.exp(-gate)) * up).astype(BF16)
        return carry

    lax.fori_loop(0, TILES, last_step, 0)
    chunks = back_go.shape[0]
    fold = BACK // MAIN

    def pack(store, values):
        for r in range(ROW_CUTS):
            at = r * PART_SLOTS
            cut = at + BLOCKS * MAIN
            blocks = slice(r * BLOCKS, (r + 1) * BLOCKS)
            for q in range(MAIN):
                fold_back[blocks, q, :] = values[cut : cut + BLOCKS, q * fold : (q + 1) * fold]
            store[blocks, :, :BACK] = values[at:cut].astype(BF16).reshape(BLOCKS, MAIN, BACK)
        store[:, :, BACK:] = fold_back[...].astype(BF16)

    def unpack(store):
        cut = EXPERTS * MAIN
        terms[:cut] = store[:, :, :BACK].reshape(cut, BACK)
        fold_back[...] = store[:, :, BACK:].astype(F32)
        for q in range(MAIN):
            terms[cut:, q * fold : (q + 1) * fold] = fold_back[:, q, :].astype(BF16)

    def back_copy(n, src, dev):
        return remote(
            back_go.at[n, dev], back_got.at[n, src], back_send.at[n, dev], back_recv.at[n, src], dev
        )

    def down_step(n, carry):
        for i in range(BACK // width):
            gather(back_raw, n * (BACK // width) + i, i * width)
        down(n).wait()
        term = jnp.dot(inner[...], dn[n % DN_SLOTS], preferred_element_type=F32)
        pack(back_go.at[n], info_ref[1, :, 0:1] * term + info_ref[0, :, 0:1] * back_raw[...])
        others(me, lambda dev: back_copy(n, me, dev).start())
        back_got[n, me] = back_go[n, me]

        @pl.when(n + DN_SLOTS < chunks)
        def _():
            down(n + DN_SLOTS).start()

        return carry

    lax.fori_loop(0, chunks, down_step, 0)

    def combine(n, carry):
        others(me, lambda dev: back_copy(n, dev, dev).wait_recv())
        unpack(back_got.at[n])
        cols = pl.ds(pl.multiple_of(n * BACK, BACK), BACK)
        out_ref[:, cols] = jnp.dot(
            place_ref[...], terms[...], preferred_element_type=F32
        ).astype(BF16)
        return carry

    lax.fori_loop(0, chunks, combine, 0)

    def finish(dev):
        hid_copy(dev).wait_send()
        ids_copy(me, dev).wait_send()
        for r in range(ROW_CUTS):
            go_copy(r, me, dev).wait_send()

        def sent(n, carry):
            back_copy(n, me, dev).wait_send()
            return carry

        lax.fori_loop(0, chunks, sent, 0)

    others(me, finish)
    for p in range(PIECES):
        for zz in range(NZ):
            @pl.when((z > 0) & (zz >= z))
            def _():
                to_left(p, zz).wait_send()

            @pl.when((z < NZ - 1) & (zz <= z))
            def _():
                to_right(p, zz).wait_send()

            to_y(p, zz).wait_send()
            to_core(p, zz, 0).wait_send()
            to_core(p, zz, 1).wait_send()


def layer(cache_len, q, ck, cv, nk, nv, out_proj, hidden, gain, router, ids, gate_proj, up_proj, down_proj):
    rows, width = q.shape
    seqs = NDEV // KVH
    cols = out_proj.shape[1]
    mine, model = hidden.shape
    ffw = gate_proj.shape[1]
    chunks = model // BACK
    tall = rows // ROW_CUTS
    span = mine * BLOCKS
    dma = pltpu.SemaphoreType.DMA
    inside = pl.BlockSpec(memory_space=pltpu.VMEM)
    outside = pl.BlockSpec(memory_space=pl.ANY)
    go = (ROW_CUTS, NDEV, PART_SLOTS, cols)
    back = (chunks, NDEV, MAIN, BACK + BACK // MAIN)
    return pl.pallas_call(
        layer_kernel,
        out_shape=jax.ShapeDtypeStruct((mine, model), BF16),
        in_specs=[pl.BlockSpec(memory_space=pltpu.SMEM)]
        + [outside] * 7
        + [inside, outside, inside]
        + [outside] * 3,
        out_specs=inside,
        scratch_shapes=[
            pltpu.VMEM(q.shape, BF16),
            pltpu.VMEM(ck.shape, BF16),
            pltpu.VMEM(cv.shape, BF16),
            pltpu.VMEM(nk.shape, BF16),
            pltpu.VMEM(nv.shape, BF16),
            pltpu.VMEM((PIECES, NDEV, tall, width // HEAD_CUTS), BF16),
            pltpu.VMEM((ROW_CUTS, seqs, tall, cols), F32),
            pltpu.VMEM((NDEV, mine, cols), BF16),
            pltpu.VMEM((NDEV, TOPK, mine), jnp.int32),
            pltpu.VMEM(out_proj.shape, BF16),
            pltpu.VMEM(router.shape, BF16),
            pltpu.VMEM((span, cols), BF16),
            pltpu.VMEM((ROW_CUTS, TOPK, span), F32),
            pltpu.VMEM((ROW_CUTS, TOPK, span), F32),
            pltpu.VMEM((ROW_CUTS, EXPERTS, PART_SLOTS, span), BF16),
            pltpu.VMEM((2, SLOTS, 128), F32),
            pltpu.VMEM((mine, SLOTS), BF16),
            pltpu.VMEM(go, BF16),
            pltpu.VMEM(go, BF16),
            pltpu.VMEM((SLOTS, 2 * cols), F32),
            pltpu.VMEM((SLOTS, 2 * cols), BF16),
            pltpu.VMEM((SLOTS, 128), F32),
            pltpu.VMEM((SLOTS, EXPERTS), F32),
            pltpu.VMEM((TILES, SLOTS, TILE), F32),
            pltpu.VMEM((TILES, SLOTS, TILE), F32),
            pltpu.VMEM((SLOTS, ffw), BF16),
            pltpu.VMEM(back, BF16),
            pltpu.VMEM(back, BF16),
            pltpu.VMEM((NDEV, MAIN, BACK // MAIN), F32),
            pltpu.VMEM((SLOTS, BACK), F32),
            pltpu.VMEM((SLOTS, BACK), BF16),
            pltpu.VMEM((GU_SLOTS, 2, 2 * cols, ffw), BF16),
            pltpu.VMEM((DN_SLOTS, ffw, BACK), BF16),
            dma((8,)), dma((GU_SLOTS, 2)), dma((DN_SLOTS,)), dma((PIECES, NDEV)),
            dma((PIECES, NZ)), dma((PIECES, NZ)), dma((PIECES, NZ)), dma((PIECES, 2 * NZ)),
            dma((NDEV,)), dma((NDEV,)), dma((NDEV,)), dma((NDEV,)),
            dma((ROW_CUTS, NDEV)), dma((ROW_CUTS, NDEV)),
            dma((chunks, NDEV)), dma((chunks, NDEV)),
        ],
        compiler_params=pltpu.CompilerParams(
            collective_id=0, has_side_effects=True, vmem_limit_bytes=63 << 20
        ),
    )(cache_len, q, ck, cv, nk, nv, out_proj, hidden, gain, router, ids, gate_proj, up_proj, down_proj)


def body(
    hidden_in, queries, cache_keys, cache_values, new_keys, new_values, cache_len,
    out_proj, norm_gain, router, expert_ids, gate_proj, up_proj, down_proj,
):
    piece, seqs, model = hidden_in.shape
    hidden = hidden_in.transpose(1, 0, 2).reshape(piece * seqs, model)
    out = layer(
        cache_len, queries[0], cache_keys[0], cache_values[0], new_keys[0], new_values[0],
        out_proj, hidden, norm_gain.reshape(1, model), router.T, expert_ids.transpose(1, 2, 0),
        gate_proj, up_proj, down_proj,
    )
    return out.reshape(seqs, piece, model).transpose(1, 0, 2)


def solution(mesh):
    placed = (
        P("ea", "rep", None),
        P(("rep", "ea"), None, None),
        P(("rep", "ea"), None, None),
        P(("rep", "ea"), None, None),
        P(("rep", "ea"), None, None),
        P(("rep", "ea"), None, None),
        P("rep"),
        P(None, "ea"),
        P(),
        P(),
        P("ea", "rep", None),
        P(None, "ea"),
        P(None, "ea"),
        P("ea", None),
    )
    plan = body if mesh.shape["ea"] == NDEV else wide_body
    return jax.shard_map(
        plan, mesh=mesh, in_specs=placed, out_specs=P("ea", "rep", None), check_vma=False
    )
```

```python
import functools
import math

import jax
import jax.numpy as jnp
from jax import lax
from jax.experimental import pallas as pl
from jax.experimental.pallas import tpu as pltpu
from jax.sharding import PartitionSpec as P

HQ = 32
KVH = 8
HD = 128
EXPERTS = 16
TOPK = 2
CAP = 9


def expert_terms(received, gate_proj, up_proj, down_proj):
    src_count, slot_count, model_width = received.shape
    flat_rows = received.reshape(src_count * slot_count, model_width)
    gate_val = jnp.dot(flat_rows, gate_proj, preferred_element_type=jnp.float32)
    up_val = jnp.dot(flat_rows, up_proj, preferred_element_type=jnp.float32)
    inner_act = (jax.nn.silu(gate_val) * up_val).astype(jnp.bfloat16)
    shard_term = jnp.dot(inner_act, down_proj, preferred_element_type=jnp.float32).astype(
        jnp.bfloat16
    )
    return shard_term.reshape(src_count, slot_count, model_width)


def expert_half(received, gate_proj, up_proj, down_proj):
    shard_term = expert_terms(received, gate_proj, up_proj, down_proj)
    return lax.all_to_all(shard_term, "ea", split_axis=0, concat_axis=0, tiled=True)


def route_rows(normed, route_ids, first_gate, gate_proj, up_proj, down_proj):
    row_count, model_width = normed.shape
    dev_count = lax.axis_size("ea")
    shard_count = dev_count // EXPERTS
    flat_ids = route_ids.reshape(-1)
    pair_count = flat_ids.shape[0]
    expert_cols = jnp.arange(EXPERTS, dtype=jnp.int32)
    one_hot = (flat_ids[:, None] == expert_cols[None, :]).astype(jnp.float32)
    pair_order = jnp.arange(pair_count, dtype=jnp.int32)
    earlier = (pair_order[:, None] > pair_order[None, :]).astype(jnp.float32)
    before = jnp.dot(earlier, one_hot, precision=lax.Precision.HIGHEST)
    slot_pos = jnp.sum(before * one_hot, axis=1).astype(jnp.int32)
    target = (flat_ids * CAP + slot_pos).reshape(row_count, TOPK)
    slot_ids = jnp.arange(EXPERTS * CAP, dtype=jnp.int32)
    select = (
        (target[None, :, 0] == slot_ids[:, None]) | (target[None, :, 1] == slot_ids[:, None])
    ).astype(jnp.bfloat16)
    packed = jnp.dot(select, normed, preferred_element_type=jnp.float32).astype(jnp.bfloat16)
    packed = jnp.broadcast_to(
        packed.reshape(EXPERTS, 1, CAP, model_width), (EXPERTS, shard_count, CAP, model_width)
    )
    packed = packed.reshape(dev_count, CAP, model_width)
    first_slots = (CAP + 1) // 2
    bounds = [(0, first_slots), (first_slots, CAP)]
    pieces = []
    for lower, upper in bounds:
        part_block = packed[:, lower:upper]
        pieces.append(
            (lambda received: expert_half(received, gate_proj, up_proj, down_proj))(
                lax.all_to_all(part_block, "ea", split_axis=0, concat_axis=0, tiled=True)
            )
        )
    returned = jnp.concatenate(pieces, axis=1)
    expert_out = jnp.sum(
        returned.reshape(EXPERTS, shard_count, CAP, model_width).astype(jnp.float32), axis=1
    )
    expert_out = expert_out.reshape(EXPERTS * CAP, model_width)
    picked = jnp.take(expert_out, target, axis=0)
    return first_gate * picked[:, 0] + (1.0 - first_gate) * picked[:, 1]


def wide_body(
    hidden_in,
    queries,
    cache_keys,
    cache_values,
    new_keys,
    new_values,
    cache_len,
    out_proj,
    norm_gain,
    router,
    expert_ids,
    gate_proj,
    up_proj,
    down_proj,
):
    dev_count = lax.axis_size("ea")
    dev_index = lax.axis_index("ea")
    new_rows = queries.shape[1]
    group_q = HQ // KVH
    seq_count = dev_count // KVH
    piece_rows = new_rows // dev_count
    cache_rows = cache_keys.shape[1]
    col_width = out_proj.shape[1]
    model_width = hidden_in.shape[2]
    score_scale = 1.0 / math.sqrt(HD)
    visible = lax.dynamic_index_in_dim(cache_len, dev_index // KVH, keepdims=False)
    position = (
        jnp.arange(new_rows, dtype=jnp.int32).reshape(dev_count, piece_rows).T.reshape(new_rows)
    )
    query_rows = (
        queries[0]
        .reshape(dev_count, piece_rows, group_q, HD)
        .transpose(1, 0, 2, 3)
        .reshape(new_rows, group_q, HD)
    )
    all_keys = jnp.concatenate([cache_keys[0], new_keys[0]], axis=0)
    all_values = jnp.concatenate([cache_values[0], new_values[0]], axis=0)
    key_pos = jnp.arange(cache_rows + new_rows, dtype=jnp.int32)
    allowed = jnp.where(
        key_pos[None, :] < cache_rows,
        key_pos[None, :] < visible,
        key_pos[None, :] - cache_rows <= position[:, None],
    )
    scores = (
        jnp.einsum("qhd,kd->hqk", query_rows, all_keys, preferred_element_type=jnp.float32)
        * score_scale
    )
    scores = jnp.where(allowed[None], scores, jnp.float32(-1e30))
    top_score = jnp.max(scores, axis=2, keepdims=True)
    exp_scores = jnp.exp(scores - top_score)
    attn_probs = (exp_scores / jnp.sum(exp_scores, axis=2, keepdims=True)).astype(jnp.bfloat16)
    attended = jnp.einsum("hqk,kd->qhd", attn_probs, all_values, preferred_element_type=jnp.float32)
    attended = attended.astype(jnp.bfloat16).reshape(new_rows, group_q * HD)
    local_rows = out_proj.reshape(KVH, group_q * HD, col_width).transpose(1, 0, 2)
    outgoing = jnp.broadcast_to(local_rows[:, None], (group_q * HD, seq_count, KVH, col_width))
    outgoing = outgoing.reshape(group_q * HD, dev_count, col_width)
    group_proj = lax.all_to_all(outgoing, "ea", split_axis=1, concat_axis=1, tiled=True).reshape(
        group_q * HD, model_width
    )
    head_part = jnp.dot(attended, group_proj, preferred_element_type=jnp.float32).astype(
        jnp.bfloat16
    )
    arrived = lax.all_to_all(
        head_part.reshape(piece_rows, dev_count, model_width),
        "ea",
        split_axis=1,
        concat_axis=1,
        tiled=True,
    )
    head_sum = jnp.sum(
        arrived.reshape(piece_rows, seq_count, KVH, model_width).astype(jnp.float32), axis=2
    )
    residual = hidden_in.astype(jnp.float32) + head_sum
    flat_res = residual.reshape(piece_rows * seq_count, model_width)
    mean_sq = jnp.mean(flat_res * flat_res, axis=1, keepdims=True)
    normed = (flat_res * lax.rsqrt(mean_sq + 1e-05) * norm_gain[None, :]).astype(jnp.bfloat16)
    logits = jnp.dot(normed, router, preferred_element_type=jnp.float32)
    route_ids = expert_ids.reshape(piece_rows * seq_count, TOPK)
    chosen = jnp.take_along_axis(logits, route_ids, axis=1)
    first_gate = jax.nn.sigmoid(chosen[:, 0:1] - chosen[:, 1:2])
    expert_mix = route_rows(normed, route_ids, first_gate, gate_proj, up_proj, down_proj)
    result_rows = (flat_res + expert_mix).astype(jnp.bfloat16)
    return result_rows.reshape(piece_rows, seq_count, model_width)


NZ = 4
NDEV = 16
MAIN = 8
SLOTS = EXPERTS * CAP
F32 = jnp.float32
BF16 = jnp.bfloat16


def attend(q, ck, cv, nk, nv, visible, first_row):
    contract = (((1,), (1,)), ((), ()))
    rows, cached, fresh = q.shape[0], ck.shape[0], nk.shape[0]
    scale = 1.0 / math.sqrt(HD)
    old = lax.dot_general(q, ck, contract, preferred_element_type=F32) * scale
    new = lax.dot_general(q, nk, contract, preferred_element_type=F32) * scale
    old_pos = lax.broadcasted_iota(jnp.int32, (rows, cached), 1)
    row_pos = lax.broadcasted_iota(jnp.int32, (rows, fresh), 0) + first_row
    new_pos = lax.broadcasted_iota(jnp.int32, (rows, fresh), 1)
    old = jnp.where(old_pos < visible, old, -1e30)
    new = jnp.where(new_pos <= row_pos, new, -1e30)
    top = jnp.maximum(
        jnp.max(old, axis=1, keepdims=True), jnp.max(new, axis=1, keepdims=True)
    )
    old = jnp.exp(old - top)
    new = jnp.exp(new - top)
    total = jnp.sum(old, axis=1, keepdims=True) + jnp.sum(new, axis=1, keepdims=True)
    mixed = jnp.dot(old.astype(BF16), cv, preferred_element_type=F32)
    mixed += jnp.dot(new.astype(BF16), nv, preferred_element_type=F32)
    return (mixed / total).astype(BF16)


def remote(src, dst, send, recv, dev):
    return pltpu.make_async_remote_copy(
        src_ref=src,
        dst_ref=dst,
        send_sem=send,
        recv_sem=recv,
        device_id={"ea": dev},
        device_id_type=pl.DeviceIdType.MESH,
    )


def greet(me):
    barrier = pltpu.get_barrier_semaphore()

    def hello(off, carry):
        pl.semaphore_signal(
            barrier,
            inc=1,
            device_id={"ea": lax.rem(me + off, NDEV)},
            device_id_type=pl.DeviceIdType.MESH,
        )
        return carry

    lax.fori_loop(1, NDEV, hello, 0)


def greeted():
    pl.semaphore_wait(pltpu.get_barrier_semaphore(), NDEV - 1)


def others(me, step):
    def go(off, carry):
        step(lax.rem(me + off, NDEV))
        return carry

    lax.fori_loop(1, NDEV, go, 0)


TILE = 640
TILES = 5
GU_SLOTS = 9
DN_SLOTS = 2
DN_COLS = 512
ROW_CUTS = 2
HEAD_CUTS = 2
PIECES = ROW_CUTS * HEAD_CUTS
BLOCKS = NDEV // ROW_CUTS
PART_SLOTS = BLOCKS * CAP
BACK = 1024


def layer_kernel(
    len_ref, q_hbm, ck_hbm, cv_hbm, nk_hbm, nv_hbm, proj_hbm, hid_hbm, gain_ref, router_hbm, ids_ref, gate_hbm, up_hbm, down_hbm,
    out_ref,
    q_ref, ck_ref, cv_ref, nk_ref, nv_ref,
    buf, acc, part_go, part_got, hid_got, ids_got, proj_ref, router_ref, resid, code_ref, name_ref, sel_ref, info_ref, place_ref,
    out_go, out_got, raw_ref, xg_ref, ss_ref, lg_ref, acts, inner, back_go, back_got, fold_back, back_raw, terms, gu, dn,
    in_sem, gu_sem, dn_sem,
    block_sem, left_sem, right_sem, core_sem, swap_send, swap_recv, part_send, part_recv,
    hid_send, hid_recv, ids_send, ids_recv, go_send, go_recv, back_send, back_recv,
):
    me = lax.axis_index("ea")
    model = gain_ref.shape[1]
    width = proj_ref.shape[3]
    quarter = proj_ref.shape[2]
    mine = hid_got.shape[1]
    piece = mine // 2
    tall, part = buf.shape[2], buf.shape[3]
    span = resid.shape[0]
    wide = gu.shape[1]
    z, y, c = me // 4, (me // 2) % 2, me % 2

    def index(zz, yy, cc):
        return (zz * 2 + yy) * 2 + cc

    def fetch(src, dst, slot):
        return pltpu.make_async_copy(src, dst, in_sem.at[slot])

    def proj_rows(q, yy):
        return proj_hbm.at[pl.ds(pl.multiple_of((q * 2 + yy) * quarter, quarter), quarter), :]

    col_me = pl.ds(pl.multiple_of(me * width, width), width)
    loads = [
        (q_hbm, q_ref), (ck_hbm, ck_ref), (nk_hbm, nk_ref), (cv_hbm, cv_ref), (nv_hbm, nv_ref),
        (proj_rows(0, y), proj_ref.at[0, 0]), (proj_rows(1, y), proj_ref.at[0, 1]),
        (hid_hbm.at[:, col_me], hid_got.at[me]), (router_hbm, router_ref),
    ]
    spare = GU_SLOTS - 2
    half_at = model // 4
    for n in range(2):
        loads.append((
            hid_hbm.at[:, n * 2 * half_at : (n + 1) * 2 * half_at],
            gu.at[spare + n, 0:mine, half_at : half_at + 2 * half_at],
        ))
    for n in range(2):
        for q in range(2):
            loads.append((
                proj_rows(q, 1 - y).at[n * wide : (n + 1) * wide],
                gu.at[spare + n, :, q * width : (q + 1) * width],
            ))
    for slot in (0, 1, 2, 3, 4, 9, 10, 11, 12, 13, 14, 5, 6, 7, 8):
        fetch(*loads[slot], slot).start()
    greet(me)

    def chip_at(s):
        low = (z + s // 2) % 2
        high = (z // 2 + s // 4) % 2
        return (high * 2 + low) * 2 + (y + s) % 2

    def gate_up(s, n):
        rows = pl.ds(pl.multiple_of(chip_at(s) * wide, wide), wide)
        slot = (2 * s + n) % GU_SLOTS
        src = (gate_hbm, up_hbm)[n]
        return pltpu.make_async_copy(src.at[rows, :], gu.at[slot], gu_sem.at[slot])

    def down(n):
        cols = pl.ds(pl.multiple_of(n * DN_COLS, DN_COLS), DN_COLS)
        slot = n % DN_SLOTS
        return pltpu.make_async_copy(down_hbm.at[:, cols], dn.at[slot], dn_sem.at[slot])

    for u in range(spare):
        gate_up(u // 2, u % 2).start()
    for n in range(DN_SLOTS):
        down(n).start()

    def hid_copy(dev):
        start = half_at + dev % (NDEV // 2) * width
        cols = pl.ds(pl.multiple_of(start, width), width)
        return remote(
            gu.at[spare + dev // (NDEV // 2), 0:mine, cols], hid_got.at[me],
            hid_send.at[dev], hid_recv.at[me], dev,
        )

    def hid_landed(dev):
        remote(
            hid_got.at[me], hid_got.at[dev], hid_send.at[dev], hid_recv.at[dev], dev
        ).wait_recv()

    def ids_copy(src, dev):
        return remote(
            ids_got.at[src], ids_got.at[src], ids_send.at[dev], ids_recv.at[src], dev
        )

    def swap(q, n):
        return remote(
            gu.at[spare + n, :, q * width : (q + 1) * width],
            proj_ref.at[1, q, n * wide : (n + 1) * wide, :],
            swap_send.at[q, n], swap_recv.at[q, n], index(z, 1 - y, c),
        )

    def share_copy(r, k):
        return remote(
            part_go.at[r, k], part_got.at[r, k], part_send.at[r, k], part_recv.at[r, k],
            index(z, 1 - y, c),
        )

    def share(r, k):
        part_go[r, k] = acc[r, k, 1].astype(BF16)
        share_copy(r, k).start()

    def block_copy(p, zz, cc, sem, dev):
        blk = zz * 2 + cc
        return remote(buf.at[p, blk], buf.at[p, blk], sem, block_sem.at[p, blk], dev)

    def to_left(p, zz):
        return block_copy(p, zz, c, left_sem.at[p, zz], index(z - 1, y, c))

    def to_right(p, zz):
        return block_copy(p, zz, c, right_sem.at[p, zz], index(z + 1, y, c))

    def to_core(p, zz):
        return block_copy(p, zz, c, core_sem.at[p, zz], index(z, y, 1 - c))

    def landed(p, zz, cc):
        block_copy(p, zz, cc, core_sem.at[p, 0], index(z, y, 1 - c)).wait_recv()

    def line(p, zz, go_left, go_right):
        if go_left:
            @pl.when(z > 0)
            def _():
                to_left(p, zz).start()
        if go_right:
            @pl.when(z < NZ - 1)
            def _():
                to_right(p, zz).start()
        to_core(p, zz).start()

    def arrive(r, d):
        for h in range(HEAD_CUTS):
            p = r * HEAD_CUTS + h

            @pl.when(z + d < NZ)
            def _():
                landed(p, z + d, c)
                line(p, z + d, True, False)

            @pl.when(z - d >= 0)
            def _():
                landed(p, z - d, c)
                line(p, z - d, False, True)

    def multiply(r, d):
        def go(n, carry):
            side, cc = n % 2, n // 2
            zz = z + d * (1 - 2 * side)
            ok = (zz >= 0) & (zz < NZ)
            if d == 0:
                ok = ok & (side == 0)

            @pl.when(ok)
            def _():
                @pl.when(cc != c)
                def _():
                    for h in range(HEAD_CUTS):
                        landed(r * HEAD_CUTS + h, zz, cc)

                k = (zz // 2 + z // 2) % 2
                for o in range(2):
                    total = acc[r, k, o]
                    for h in range(HEAD_CUTS):
                        start = (cc * HEAD_CUTS + h) * part
                        rows = pl.ds(pl.multiple_of(start, part), part)
                        total += jnp.dot(
                            buf[r * HEAD_CUTS + h, zz * 2 + cc],
                            proj_ref[o, zz % 2, rows, :],
                            preferred_element_type=F32,
                        )
                    acc[r, k, o] = total

            return carry

        lax.fori_loop(0, 4, go, 0)

    for slot in range(5):
        fetch(*loads[slot], slot).wait()
    visible = len_ref[me // KVH]

    def attention(r, h):
        keys = slice(0, (r + 1) * tall)

        def head(n, carry):
            src = pl.ds(pl.multiple_of(h * part + n * HD, HD), HD)
            dst = pl.ds(pl.multiple_of(n * HD, HD), HD)
            buf[r * HEAD_CUTS + h, z * 2 + c, :, dst] = attend(
                q_ref[r * tall : (r + 1) * tall, src], ck_ref[...], cv_ref[...],
                nk_ref[keys], nv_ref[keys], visible, r * tall,
            )
            return carry

        lax.fori_loop(0, part // HD, head, 0)

    ids_got[me] = jnp.concatenate([ids_ref[0], ids_ref[1]], axis=1)
    attention(0, 0)
    greeted()
    line(0, z, True, True)
    for slot in range(9, 15):
        fetch(*loads[slot], slot).wait()
    for q in range(2):
        for n in range(2):
            swap(q, n).start()
    others(me, lambda dev: ids_copy(me, dev).start())
    others(me, lambda dev: hid_copy(dev).start())
    for r in range(ROW_CUTS):
        for h in range(HEAD_CUTS):
            if r or h:
                attention(r, h)
                line(r * HEAD_CUTS + h, z, True, True)
    acc[...] = jnp.zeros_like(acc)
    acts[...] = jnp.zeros_like(acts)
    ss_ref[...] = jnp.zeros_like(ss_ref)
    lg_ref[...] = jnp.zeros_like(lg_ref)

    def ranks(ids, block):
        lanes = ids.shape[1]
        rows = lax.broadcasted_iota(jnp.int32, (EXPERTS, lanes), 0)
        first = (ids[0:1] == rows).astype(F32)
        second = (ids[1:2] == rows).astype(F32)
        one = lax.broadcasted_iota(jnp.int32, (lanes, lanes), 0)
        two = lax.broadcasted_iota(jnp.int32, (lanes, lanes), 1)
        same = (one // block) == (two // block)
        tri = ((one < two) & same).astype(F32)
        before0 = jnp.dot(first, tri, preferred_element_type=F32)
        before1 = jnp.dot(second, tri, preferred_element_type=F32) + jnp.dot(
            first, same.astype(F32), preferred_element_type=F32
        )
        return (
            jnp.sum(before0 * first, axis=0, keepdims=True),
            jnp.sum(before1 * second, axis=0, keepdims=True),
        )

    def own_places():
        ids = ids_got[me]
        spots = lax.broadcasted_iota(jnp.int32, (SLOTS, mine), 0).astype(F32)
        total = jnp.zeros((SLOTS, mine), F32)
        for k, rank in enumerate(ranks(ids, mine)):
            expert = ids[k : k + 1].astype(F32)
            where = jnp.where(rank < MAIN - 0.5, expert * MAIN + rank, EXPERTS * MAIN + expert)
            total += (spots == where).astype(F32)
        place_ref[...] = total.T.astype(BF16)

    def codes():
        others(me, lambda dev: ids_copy(dev, dev).wait_recv())
        for q in range(NDEV // 2):
            ids = jnp.concatenate([ids_got[2 * q], ids_got[2 * q + 1]], axis=1)
            r, at = 2 * q // BLOCKS, (2 * q % BLOCKS) * mine
            lane = lax.broadcasted_iota(jnp.int32, (1, 2 * mine), 1)
            block = ((at + lane) // mine).astype(F32)
            cols = slice(at, at + 2 * mine)
            for k, rank in enumerate(ranks(ids, mine)):
                name = ids[k : k + 1].astype(F32)
                spot = jnp.where(rank < MAIN - 0.5, block * MAIN + rank, BLOCKS * MAIN + block)
                code_ref[r, k : k + 1, cols] = name * PART_SLOTS + spot
                name_ref[r, k : k + 1, cols] = name

    def spots_of(e):
        rows = lax.broadcasted_iota(jnp.int32, (PART_SLOTS, span), 0)
        return (rows + e * PART_SLOTS).astype(F32)

    def selects(r):
        def go(e, carry):
            spots = spots_of(e)
            hit = (spots == code_ref[r, 0:1, :]) | (spots == code_ref[r, 1:2, :])
            sel_ref[r, e] = hit.astype(F32).astype(BF16)
            return carry

        lax.fori_loop(0, EXPERTS, go, 0)

    def infos():
        for r in range(ROW_CUTS):
            spots = spots_of(me)
            hit0 = (spots == code_ref[r, 0:1, :]).astype(F32)
            hit1 = (spots == code_ref[r, 1:2, :]).astype(F32)
            chosen = jnp.sum(hit0, axis=1, keepdims=True)
            other = jnp.sum(
                hit0 * name_ref[r, 1:2, :] + hit1 * name_ref[r, 0:1, :], axis=1, keepdims=True
            )
            rows = slice(r * PART_SLOTS, (r + 1) * PART_SLOTS)
            info_ref[0, rows, :] = jnp.broadcast_to(chosen, (PART_SLOTS, info_ref.shape[2]))
            info_ref[1, rows, :] = jnp.broadcast_to(other, (PART_SLOTS, info_ref.shape[2]))

    def go_copy(r, src, dev):
        return remote(
            out_go.at[r, dev], out_got.at[r, src], go_send.at[r, dev], go_recv.at[r, src], dev
        )

    def residual(r):
        for b in range(BLOCKS):
            for s in range(2):
                rows = slice(b * piece, (b + 1) * piece)
                at = b * mine + s * piece
                k = (s + z // 2) % 2
                value = acc[r, k, 0, rows, :] + part_got[r, k, rows, :].astype(F32)
                value += hid_got[r * BLOCKS + b, s * piece : (s + 1) * piece, :].astype(F32)
                resid[at : at + piece, :] = value.astype(BF16)

    def select(r, dev):
        return jnp.dot(sel_ref[r, dev], resid[...], preferred_element_type=F32).astype(BF16)

    def first_send(i, carry):
        dev = (me + 7 * i) % NDEV
        out_go[0, dev] = select(0, dev)
        go_copy(0, me, dev).start()
        return carry

    def last_sends(s, step):
        for n in range(2):
            dev = chip_at(s) * 2 + n
            if isinstance(s, int) and s == 0:
                @pl.when(dev != me)
                def _():
                    step(go_copy(1, me, dev))
            else:
                step(go_copy(1, me, dev))

    def last_select(s):
        for n in range(2):
            dev = chip_at(s) * 2 + n
            out_go[1, dev] = select(1, dev)

    arrive(0, 1)
    own_places()
    arrive(1, 1)
    codes()
    arrive(0, 2)
    selects(0)
    infos()
    arrive(1, 2)
    for q in range(2):
        fetch(*loads[5 + q], 5 + q).wait()
        for n in range(2):
            swap(q, n).wait()
    others(me, lambda dev: hid_copy(dev).wait_send())
    for u in range(spare, GU_SLOTS):
        gate_up(u // 2, u % 2).start()
    multiply(0, 0)
    multiply(0, 1)
    share(0, 0)
    selects(1)
    arrive(0, 3)
    multiply(0, 2)
    multiply(0, 3)
    share(0, 1)
    multiply(1, 0)
    multiply(1, 1)
    share(1, 0)
    others(me, hid_landed)
    fetch(*loads[7], 7).wait()
    for k in range(2):
        share_copy(0, k).wait_recv()
    residual(0)
    lax.fori_loop(1, NDEV, first_send, 0)
    out_got[0, me] = select(0, me)
    arrive(1, 3)
    multiply(1, 2)
    multiply(1, 3)
    share(1, 1)
    for k in range(2):
        share_copy(1, k).wait_recv()
    residual(1)
    for s in (4, 5, 1, 2, 3, 0, 6, 7):
        last_select(s)
        if s < 6:
            last_sends(s, lambda copy: copy.start())
    out_got[1, me] = out_go[1, me]
    fetch(*loads[8], 8).wait()

    def gather(ref, dev, at):
        for r in range(ROW_CUTS):
            rows = slice(r * PART_SLOTS, (r + 1) * PART_SLOTS)
            ref[rows, at : at + width] = out_got[r, dev].astype(F32)

    steps = model // wide

    def take(s):
        chip = chip_at(s)
        for n in range(2):
            dev = chip * 2 + n

            @pl.when(dev != me)
            def _():
                for r in range(ROW_CUTS):
                    go_copy(r, dev, dev).wait_recv()

            gather(raw_ref, dev, n * width)
        raw = raw_ref[...]
        cols = pl.ds(pl.multiple_of(chip * wide, wide), wide)
        xg_ref[...] = (raw * gain_ref[:, cols]).astype(BF16)
        ss_ref[...] += jnp.broadcast_to(jnp.sum(raw * raw, axis=1, keepdims=True), ss_ref.shape)
        lg_ref[...] += lax.dot_general(
            xg_ref[...], router_ref[:, cols], (((1,), (1,)), ((), ())), preferred_element_type=F32
        )
        for n in range(2):
            gate_up(s, n).wait()

    def products(s):
        def one(n, carry):
            acts[n] += jnp.dot(
                xg_ref[...], gu[(2 * s + n) % GU_SLOTS], preferred_element_type=F32
            )
            return carry

        lax.fori_loop(0, 2, one, 0)

    def expert_step(s, carry):
        @pl.when((s == 2) | (s == 3))
        def _():
            last_sends(s + 2, lambda copy: copy.wait_send())
            last_sends(s + 4, lambda copy: copy.start())

        take(s)
        products(s)

        for n in range(2):
            at = 2 * s + n + GU_SLOTS

            @pl.when(at < 2 * steps)
            def _():
                gate_up(s + (n + GU_SLOTS) // 2, (n + GU_SLOTS) % 2).start()

        return carry

    lax.fori_loop(0, steps - 1, expert_step, 0)
    take(steps - 1)
    products(steps - 1)
    scale = lax.rsqrt(ss_ref[:, 0:1] / model + 1e-05)
    names = lax.broadcasted_iota(jnp.int32, lg_ref.shape, 1).astype(F32)
    mine_at = (names == me.astype(F32)).astype(F32)
    other_at = (names == info_ref[1, :, 0:1]).astype(F32)
    gap = jnp.sum(lg_ref[...] * (mine_at - other_at), axis=1, keepdims=True) * scale
    info_ref[1] = jnp.broadcast_to(jax.nn.sigmoid(gap), info_ref.shape[1:])

    def last_step(t, carry):
        cols = pl.ds(pl.multiple_of(t * TILE, TILE), TILE)
        gate, up = acts[0, :, cols] * scale, acts[1, :, cols] * scale
        inner[:, cols] = (gate / (1.0 + jnp.exp(-gate)) * up).astype(BF16)
        return carry

    lax.fori_loop(0, TILES, last_step, 0)
    chunks = back_go.shape[0]
    fold = BACK // MAIN

    def pack(store, values):
        for r in range(ROW_CUTS):
            at = r * PART_SLOTS
            cut = at + BLOCKS * MAIN
            blocks = slice(r * BLOCKS, (r + 1) * BLOCKS)
            for q in range(MAIN):
                fold_back[blocks, q, :] = values[cut : cut + BLOCKS, q * fold : (q + 1) * fold]
            store[blocks, :, :BACK] = values[at:cut].astype(BF16).reshape(BLOCKS, MAIN, BACK)
        store[:, :, BACK:] = fold_back[...].astype(BF16)

    def unpack(store):
        cut = EXPERTS * MAIN
        terms[:cut] = store[:, :, :BACK].reshape(cut, BACK)
        fold_back[...] = store[:, :, BACK:].astype(F32)
        for q in range(MAIN):
            terms[cut:, q * fold : (q + 1) * fold] = fold_back[:, q, :].astype(BF16)

    def back_copy(n, src, dev):
        return remote(
            back_go.at[n, dev], back_got.at[n, src], back_send.at[n, dev], back_recv.at[n, src], dev
        )

    def down_step(n, carry):
        for i in range(BACK // width):
            gather(back_raw, n * (BACK // width) + i, i * width)
        for i in range(DN_SLOTS):
            m = n * DN_SLOTS + i
            down(m).wait()
            cols = slice(i * DN_COLS, (i + 1) * DN_COLS)
            term = jnp.dot(inner[...], dn[i], preferred_element_type=F32)
            back_raw[:, cols] = (
                info_ref[1, :, 0:1] * term + info_ref[0, :, 0:1] * back_raw[:, cols]
            )

            @pl.when(n + 1 < chunks)
            def _():
                down(m + DN_SLOTS).start()

        pack(back_go.at[n], back_raw)
        others(me, lambda dev: back_copy(n, me, dev).start())
        back_got[n, me] = back_go[n, me]
        return carry

    lax.fori_loop(0, chunks, down_step, 0)

    def combine(n, carry):
        others(me, lambda dev: back_copy(n, dev, dev).wait_recv())
        unpack(back_got.at[n])
        cols = pl.ds(pl.multiple_of(n * BACK, BACK), BACK)
        out_ref[:, cols] = jnp.dot(
            place_ref[...], terms[...], preferred_element_type=F32
        ).astype(BF16)
        return carry

    lax.fori_loop(0, chunks, combine, 0)

    def finish(dev):
        ids_copy(me, dev).wait_send()
        go_copy(0, me, dev).wait_send()

        def sent(n, carry):
            back_copy(n, me, dev).wait_send()
            return carry

        lax.fori_loop(0, chunks, sent, 0)

    others(me, finish)
    for s in (0, 1, 2, 3, 6, 7):
        last_sends(s, lambda copy: copy.wait_send())
    for r in range(ROW_CUTS):
        for k in range(2):
            share_copy(r, k).wait_send()
    for p in range(PIECES):
        for zz in range(NZ):
            @pl.when((z > 0) & (zz >= z))
            def _():
                to_left(p, zz).wait_send()

            @pl.when((z < NZ - 1) & (zz <= z))
            def _():
                to_right(p, zz).wait_send()

            to_core(p, zz).wait_send()


def layer(cache_len, q, ck, cv, nk, nv, out_proj, hidden, gain, router, ids, gate_proj, up_proj, down_proj):
    rows, width = q.shape
    seqs = NDEV // KVH
    cols = out_proj.shape[1]
    mine, model = hidden.shape
    ffw = gate_proj.shape[1]
    chunks = model // BACK
    tall = rows // ROW_CUTS
    span = mine * BLOCKS
    dma = pltpu.SemaphoreType.DMA
    inside = pl.BlockSpec(memory_space=pltpu.VMEM)
    outside = pl.BlockSpec(memory_space=pl.ANY)
    go = (ROW_CUTS, NDEV, PART_SLOTS, cols)
    back = (chunks, NDEV, MAIN, BACK + BACK // MAIN)
    return pl.pallas_call(
        layer_kernel,
        out_shape=jax.ShapeDtypeStruct((mine, model), BF16),
        in_specs=[pl.BlockSpec(memory_space=pltpu.SMEM)]
        + [outside] * 7
        + [inside, outside, inside]
        + [outside] * 3,
        out_specs=inside,
        scratch_shapes=[
            pltpu.VMEM(q.shape, BF16),
            pltpu.VMEM(ck.shape, BF16),
            pltpu.VMEM(cv.shape, BF16),
            pltpu.VMEM(nk.shape, BF16),
            pltpu.VMEM(nv.shape, BF16),
            pltpu.VMEM((PIECES, 2 * NZ, tall, width // HEAD_CUTS), BF16),
            pltpu.VMEM((ROW_CUTS, seqs, 2, tall, cols), F32),
            pltpu.VMEM((ROW_CUTS, seqs, tall, cols), BF16),
            pltpu.VMEM((ROW_CUTS, seqs, tall, cols), BF16),
            pltpu.VMEM((NDEV, mine, cols), BF16),
            pltpu.VMEM((NDEV, TOPK, mine), jnp.int32),
            pltpu.VMEM((2, 2, out_proj.shape[0] // 4, cols), BF16),
            pltpu.VMEM(router.shape, BF16),
            pltpu.VMEM((span, cols), BF16),
            pltpu.VMEM((ROW_CUTS, TOPK, span), F32),
            pltpu.VMEM((ROW_CUTS, TOPK, span), F32),
            pltpu.VMEM((ROW_CUTS, EXPERTS, PART_SLOTS, span), BF16),
            pltpu.VMEM((2, SLOTS, 128), F32),
            pltpu.VMEM((mine, SLOTS), BF16),
            pltpu.VMEM(go, BF16),
            pltpu.VMEM(go, BF16),
            pltpu.VMEM((SLOTS, 2 * cols), F32),
            pltpu.VMEM((SLOTS, 2 * cols), BF16),
            pltpu.VMEM((SLOTS, 128), F32),
            pltpu.VMEM((SLOTS, EXPERTS), F32),
            pltpu.VMEM((2, SLOTS, ffw), F32),
            pltpu.VMEM((SLOTS, ffw), BF16),
            pltpu.VMEM(back, BF16),
            pltpu.VMEM(back, BF16),
            pltpu.VMEM((NDEV, MAIN, BACK // MAIN), F32),
            pltpu.VMEM((SLOTS, BACK), F32),
            pltpu.VMEM((SLOTS, BACK), BF16),
            pltpu.VMEM((GU_SLOTS, 2 * cols, ffw), BF16),
            pltpu.VMEM((DN_SLOTS, ffw, DN_COLS), BF16),
            dma((15,)), dma((GU_SLOTS,)), dma((DN_SLOTS,)), dma((PIECES, 2 * NZ)),
            dma((PIECES, NZ)), dma((PIECES, NZ)), dma((PIECES, NZ)), dma((2, 2)), dma((2, 2)),
            dma((ROW_CUTS, seqs)), dma((ROW_CUTS, seqs)),
            dma((NDEV,)), dma((NDEV,)), dma((NDEV,)), dma((NDEV,)),
            dma((ROW_CUTS, NDEV)), dma((ROW_CUTS, NDEV)),
            dma((chunks, NDEV)), dma((chunks, NDEV)),
        ],
        compiler_params=pltpu.CompilerParams(
            collective_id=0, has_side_effects=True, vmem_limit_bytes=63 << 20
        ),
    )(cache_len, q, ck, cv, nk, nv, out_proj, hidden, gain, router, ids, gate_proj, up_proj, down_proj)


def body(
    hidden_in, queries, cache_keys, cache_values, new_keys, new_values, cache_len,
    out_proj, norm_gain, router, expert_ids, gate_proj, up_proj, down_proj,
):
    piece, seqs, model = hidden_in.shape
    hidden = hidden_in.transpose(1, 0, 2).reshape(piece * seqs, model)
    out = layer(
        cache_len, queries[0], cache_keys[0], cache_values[0], new_keys[0], new_values[0],
        out_proj, hidden, norm_gain.reshape(1, model), router.T, expert_ids.transpose(1, 2, 0),
        gate_proj, up_proj, down_proj,
    )
    return out.reshape(seqs, piece, model).transpose(1, 0, 2)


def solution(mesh):
    placed = (
        P("ea", "rep", None),
        P(("rep", "ea"), None, None),
        P(("rep", "ea"), None, None),
        P(("rep", "ea"), None, None),
        P(("rep", "ea"), None, None),
        P(("rep", "ea"), None, None),
        P("rep"),
        P(None, "ea"),
        P(),
        P(),
        P("ea", "rep", None),
        P(None, "ea"),
        P(None, "ea"),
        P("ea", None),
    )
    plan = body if mesh.shape["ea"] == NDEV else wide_body
    return jax.shard_map(
        plan, mesh=mesh, in_specs=placed, out_specs=P("ea", "rep", None), check_vma=False
    )
```

```python
import functools
import math

import jax
import jax.numpy as jnp
from jax import lax
from jax.experimental import pallas as pl
from jax.experimental.pallas import tpu as pltpu
from jax.sharding import PartitionSpec as P

HQ = 32
KVH = 8
HD = 128
EXPERTS = 16
TOPK = 2
CAP = 9


def expert_terms(received, gate_proj, up_proj, down_proj):
    src_count, slot_count, model_width = received.shape
    flat_rows = received.reshape(src_count * slot_count, model_width)
    gate_val = jnp.dot(flat_rows, gate_proj, preferred_element_type=jnp.float32)
    up_val = jnp.dot(flat_rows, up_proj, preferred_element_type=jnp.float32)
    inner_act = (jax.nn.silu(gate_val) * up_val).astype(jnp.bfloat16)
    shard_term = jnp.dot(inner_act, down_proj, preferred_element_type=jnp.float32).astype(
        jnp.bfloat16
    )
    return shard_term.reshape(src_count, slot_count, model_width)


def expert_half(received, gate_proj, up_proj, down_proj):
    shard_term = expert_terms(received, gate_proj, up_proj, down_proj)
    return lax.all_to_all(shard_term, "ea", split_axis=0, concat_axis=0, tiled=True)


def route_rows(normed, route_ids, first_gate, gate_proj, up_proj, down_proj):
    row_count, model_width = normed.shape
    dev_count = lax.axis_size("ea")
    shard_count = dev_count // EXPERTS
    flat_ids = route_ids.reshape(-1)
    pair_count = flat_ids.shape[0]
    expert_cols = jnp.arange(EXPERTS, dtype=jnp.int32)
    one_hot = (flat_ids[:, None] == expert_cols[None, :]).astype(jnp.float32)
    pair_order = jnp.arange(pair_count, dtype=jnp.int32)
    earlier = (pair_order[:, None] > pair_order[None, :]).astype(jnp.float32)
    before = jnp.dot(earlier, one_hot, precision=lax.Precision.HIGHEST)
    slot_pos = jnp.sum(before * one_hot, axis=1).astype(jnp.int32)
    target = (flat_ids * CAP + slot_pos).reshape(row_count, TOPK)
    slot_ids = jnp.arange(EXPERTS * CAP, dtype=jnp.int32)
    select = (
        (target[None, :, 0] == slot_ids[:, None]) | (target[None, :, 1] == slot_ids[:, None])
    ).astype(jnp.bfloat16)
    packed = jnp.dot(select, normed, preferred_element_type=jnp.float32).astype(jnp.bfloat16)
    packed = jnp.broadcast_to(
        packed.reshape(EXPERTS, 1, CAP, model_width), (EXPERTS, shard_count, CAP, model_width)
    )
    packed = packed.reshape(dev_count, CAP, model_width)
    first_slots = (CAP + 1) // 2
    bounds = [(0, first_slots), (first_slots, CAP)]
    pieces = []
    for lower, upper in bounds:
        part_block = packed[:, lower:upper]
        pieces.append(
            (lambda received: expert_half(received, gate_proj, up_proj, down_proj))(
                lax.all_to_all(part_block, "ea", split_axis=0, concat_axis=0, tiled=True)
            )
        )
    returned = jnp.concatenate(pieces, axis=1)
    expert_out = jnp.sum(
        returned.reshape(EXPERTS, shard_count, CAP, model_width).astype(jnp.float32), axis=1
    )
    expert_out = expert_out.reshape(EXPERTS * CAP, model_width)
    picked = jnp.take(expert_out, target, axis=0)
    return first_gate * picked[:, 0] + (1.0 - first_gate) * picked[:, 1]


def wide_body(
    hidden_in,
    queries,
    cache_keys,
    cache_values,
    new_keys,
    new_values,
    cache_len,
    out_proj,
    norm_gain,
    router,
    expert_ids,
    gate_proj,
    up_proj,
    down_proj,
):
    dev_count = lax.axis_size("ea")
    dev_index = lax.axis_index("ea")
    new_rows = queries.shape[1]
    group_q = HQ // KVH
    seq_count = dev_count // KVH
    piece_rows = new_rows // dev_count
    cache_rows = cache_keys.shape[1]
    col_width = out_proj.shape[1]
    model_width = hidden_in.shape[2]
    score_scale = 1.0 / math.sqrt(HD)
    visible = lax.dynamic_index_in_dim(cache_len, dev_index // KVH, keepdims=False)
    position = (
        jnp.arange(new_rows, dtype=jnp.int32).reshape(dev_count, piece_rows).T.reshape(new_rows)
    )
    query_rows = (
        queries[0]
        .reshape(dev_count, piece_rows, group_q, HD)
        .transpose(1, 0, 2, 3)
        .reshape(new_rows, group_q, HD)
    )
    all_keys = jnp.concatenate([cache_keys[0], new_keys[0]], axis=0)
    all_values = jnp.concatenate([cache_values[0], new_values[0]], axis=0)
    key_pos = jnp.arange(cache_rows + new_rows, dtype=jnp.int32)
    allowed = jnp.where(
        key_pos[None, :] < cache_rows,
        key_pos[None, :] < visible,
        key_pos[None, :] - cache_rows <= position[:, None],
    )
    scores = (
        jnp.einsum("qhd,kd->hqk", query_rows, all_keys, preferred_element_type=jnp.float32)
        * score_scale
    )
    scores = jnp.where(allowed[None], scores, jnp.float32(-1e30))
    top_score = jnp.max(scores, axis=2, keepdims=True)
    exp_scores = jnp.exp(scores - top_score)
    attn_probs = (exp_scores / jnp.sum(exp_scores, axis=2, keepdims=True)).astype(jnp.bfloat16)
    attended = jnp.einsum("hqk,kd->qhd", attn_probs, all_values, preferred_element_type=jnp.float32)
    attended = attended.astype(jnp.bfloat16).reshape(new_rows, group_q * HD)
    local_rows = out_proj.reshape(KVH, group_q * HD, col_width).transpose(1, 0, 2)
    outgoing = jnp.broadcast_to(local_rows[:, None], (group_q * HD, seq_count, KVH, col_width))
    outgoing = outgoing.reshape(group_q * HD, dev_count, col_width)
    group_proj = lax.all_to_all(outgoing, "ea", split_axis=1, concat_axis=1, tiled=True).reshape(
        group_q * HD, model_width
    )
    head_part = jnp.dot(attended, group_proj, preferred_element_type=jnp.float32).astype(
        jnp.bfloat16
    )
    arrived = lax.all_to_all(
        head_part.reshape(piece_rows, dev_count, model_width),
        "ea",
        split_axis=1,
        concat_axis=1,
        tiled=True,
    )
    head_sum = jnp.sum(
        arrived.reshape(piece_rows, seq_count, KVH, model_width).astype(jnp.float32), axis=2
    )
    residual = hidden_in.astype(jnp.float32) + head_sum
    flat_res = residual.reshape(piece_rows * seq_count, model_width)
    mean_sq = jnp.mean(flat_res * flat_res, axis=1, keepdims=True)
    normed = (flat_res * lax.rsqrt(mean_sq + 1e-05) * norm_gain[None, :]).astype(jnp.bfloat16)
    logits = jnp.dot(normed, router, preferred_element_type=jnp.float32)
    route_ids = expert_ids.reshape(piece_rows * seq_count, TOPK)
    chosen = jnp.take_along_axis(logits, route_ids, axis=1)
    first_gate = jax.nn.sigmoid(chosen[:, 0:1] - chosen[:, 1:2])
    expert_mix = route_rows(normed, route_ids, first_gate, gate_proj, up_proj, down_proj)
    result_rows = (flat_res + expert_mix).astype(jnp.bfloat16)
    return result_rows.reshape(piece_rows, seq_count, model_width)


NZ = 4
NDEV = 16
MAIN = 8
SLOTS = EXPERTS * CAP
F32 = jnp.float32
BF16 = jnp.bfloat16


def attend(q, ck, cv, nk, nv, visible, first_row):
    contract = (((1,), (1,)), ((), ()))
    rows, cached, fresh = q.shape[0], ck.shape[0], nk.shape[0]
    scale = 1.0 / math.sqrt(HD)
    old = lax.dot_general(q, ck, contract, preferred_element_type=F32) * scale
    new = lax.dot_general(q, nk, contract, preferred_element_type=F32) * scale
    old_pos = lax.broadcasted_iota(jnp.int32, (rows, cached), 1)
    row_pos = lax.broadcasted_iota(jnp.int32, (rows, fresh), 0) + first_row
    new_pos = lax.broadcasted_iota(jnp.int32, (rows, fresh), 1)
    old = jnp.where(old_pos < visible, old, -1e30)
    new = jnp.where(new_pos <= row_pos, new, -1e30)
    top = jnp.maximum(
        jnp.max(old, axis=1, keepdims=True), jnp.max(new, axis=1, keepdims=True)
    )
    old = jnp.exp(old - top)
    new = jnp.exp(new - top)
    total = jnp.sum(old, axis=1, keepdims=True) + jnp.sum(new, axis=1, keepdims=True)
    mixed = jnp.dot(old.astype(BF16), cv, preferred_element_type=F32)
    mixed += jnp.dot(new.astype(BF16), nv, preferred_element_type=F32)
    return (mixed / total).astype(BF16)


def remote(src, dst, send, recv, dev):
    return pltpu.make_async_remote_copy(
        src_ref=src,
        dst_ref=dst,
        send_sem=send,
        recv_sem=recv,
        device_id={"ea": dev},
        device_id_type=pl.DeviceIdType.MESH,
    )


def greet(me):
    barrier = pltpu.get_barrier_semaphore()

    def hello(off, carry):
        pl.semaphore_signal(
            barrier,
            inc=1,
            device_id={"ea": lax.rem(me + off, NDEV)},
            device_id_type=pl.DeviceIdType.MESH,
        )
        return carry

    lax.fori_loop(1, NDEV, hello, 0)


def greeted():
    pl.semaphore_wait(pltpu.get_barrier_semaphore(), NDEV - 1)


def others(me, step):
    def go(off, carry):
        step(lax.rem(me + off, NDEV))
        return carry

    lax.fori_loop(1, NDEV, go, 0)


TILE = 640
TILES = 5
GU_SLOTS = 9
DN_SLOTS = 2
DN_COLS = 512
ROW_CUTS = 2
HEAD_CUTS = 2
PIECES = ROW_CUTS * HEAD_CUTS
BLOCKS = NDEV // ROW_CUTS
PART_SLOTS = BLOCKS * CAP
BACK = 1024


def layer_kernel(
    len_ref, q_hbm, ck_hbm, cv_hbm, nk_hbm, nv_hbm, proj_hbm, hid_hbm, gain_ref, router_hbm, ids_ref, gate_hbm, up_hbm, down_hbm,
    out_ref,
    q_ref, ck_ref, cv_ref, nk_ref, nv_ref,
    buf, acc, part_go, part_got, hid_raw, hid_got, ids_got, proj_ref, router_ref, resid, code_ref, name_ref, sel_ref, info_ref, place_ref,
    out_go, out_got, raw_ref, xg_ref, ss_ref, lg_ref, acts, inner, back_go, back_got, fold_back, back_raw, terms, gu, dn,
    in_sem, gu_sem, dn_sem,
    block_sem, left_sem, right_sem, core_sem, swap_send, swap_recv, part_send, part_recv,
    hid_send, hid_recv, ids_send, ids_recv, go_send, go_recv, back_send, back_recv,
):
    me = lax.axis_index("ea")
    model = gain_ref.shape[1]
    width = proj_ref.shape[3]
    quarter = proj_ref.shape[2]
    mine = hid_got.shape[1]
    piece = mine // 2
    tall, part = buf.shape[2], buf.shape[3]
    span = resid.shape[0]
    wide = gu.shape[1]
    z, y, c = me // 4, (me // 2) % 2, me % 2

    def index(zz, yy, cc):
        return (zz * 2 + yy) * 2 + cc

    def fetch(src, dst, slot):
        return pltpu.make_async_copy(src, dst, in_sem.at[slot])

    def proj_rows(q, yy):
        return proj_hbm.at[pl.ds(pl.multiple_of((q * 2 + yy) * quarter, quarter), quarter), :]

    def order():
        rows = lax.broadcasted_iota(jnp.int32, (mine, mine), 0)
        source = 2 * (rows % piece) + rows // piece
        lanes = lax.broadcasted_iota(jnp.int32, (mine, mine), 1)
        return (lanes == source).astype(F32).astype(BF16)

    loads = [
        (q_hbm, q_ref), (ck_hbm, ck_ref), (nk_hbm, nk_ref), (cv_hbm, cv_ref), (nv_hbm, nv_ref),
        (proj_rows(0, y), proj_ref.at[0, 0]), (proj_rows(1, y), proj_ref.at[0, 1]),
        (hid_hbm, hid_raw), (router_hbm, router_ref),
    ]
    spare = GU_SLOTS - 2
    half_at = model // 4
    for n in range(2):
        for q in range(2):
            loads.append((
                proj_rows(q, 1 - y).at[n * wide : (n + 1) * wide],
                gu.at[spare + n, :, q * width : (q + 1) * width],
            ))
    for slot in (0, 1, 2, 3, 4, 7, 9, 10, 11, 12, 5, 6, 8):
        fetch(*loads[slot], slot).start()
    greet(me)

    def chip_at(s):
        low = (z + s // 2) % 2
        high = (z // 2 + s // 4) % 2
        return (high * 2 + low) * 2 + (y + s) % 2

    def gate_up(s, n):
        rows = pl.ds(pl.multiple_of(chip_at(s) * wide, wide), wide)
        slot = (2 * s + n) % GU_SLOTS
        src = (gate_hbm, up_hbm)[n]
        return pltpu.make_async_copy(src.at[rows, :], gu.at[slot], gu_sem.at[slot])

    def down(n):
        cols = pl.ds(pl.multiple_of(n * DN_COLS, DN_COLS), DN_COLS)
        slot = n % DN_SLOTS
        return pltpu.make_async_copy(down_hbm.at[:, cols], dn.at[slot], dn_sem.at[slot])

    for u in range(spare):
        gate_up(u // 2, u % 2).start()
    for n in range(DN_SLOTS):
        down(n).start()

    def hid_copy(dev):
        start = half_at + dev % (NDEV // 2) * width
        cols = pl.ds(pl.multiple_of(start, width), width)
        return remote(
            gu.at[spare + dev // (NDEV // 2), 0:mine, cols], hid_got.at[me],
            hid_send.at[dev], hid_recv.at[me], dev,
        )

    def hid_landed(dev):
        remote(
            hid_got.at[me], hid_got.at[dev], hid_send.at[dev], hid_recv.at[dev], dev
        ).wait_recv()

    def ids_copy(src, dev):
        return remote(
            ids_got.at[src], ids_got.at[src], ids_send.at[dev], ids_recv.at[src], dev
        )

    def swap(q, n):
        return remote(
            gu.at[spare + n, :, q * width : (q + 1) * width],
            proj_ref.at[1, q, n * wide : (n + 1) * wide, :],
            swap_send.at[q, n], swap_recv.at[q, n], index(z, 1 - y, c),
        )

    def share_copy(r, k):
        return remote(
            part_go.at[r, k], part_got.at[r, k], part_send.at[r, k], part_recv.at[r, k],
            index(z, 1 - y, c),
        )

    def share(r, k):
        part_go[r, k] = acc[r, k, 1].astype(BF16)
        share_copy(r, k).start()

    def block_copy(p, zz, cc, sem, dev):
        blk = zz * 2 + cc
        return remote(buf.at[p, blk], buf.at[p, blk], sem, block_sem.at[p, blk], dev)

    def to_left(p, zz):
        return block_copy(p, zz, c, left_sem.at[p, zz], index(z - 1, y, c))

    def to_right(p, zz):
        return block_copy(p, zz, c, right_sem.at[p, zz], index(z + 1, y, c))

    def to_core(p, zz):
        return block_copy(p, zz, c, core_sem.at[p, zz], index(z, y, 1 - c))

    def landed(p, zz, cc):
        block_copy(p, zz, cc, core_sem.at[p, 0], index(z, y, 1 - c)).wait_recv()

    def line(p, zz, go_left, go_right):
        if go_left:
            @pl.when(z > 0)
            def _():
                to_left(p, zz).start()
        if go_right:
            @pl.when(z < NZ - 1)
            def _():
                to_right(p, zz).start()
        to_core(p, zz).start()

    def arrive(r, d):
        for h in range(HEAD_CUTS):
            p = r * HEAD_CUTS + h

            @pl.when(z + d < NZ)
            def _():
                landed(p, z + d, c)
                line(p, z + d, True, False)

            @pl.when(z - d >= 0)
            def _():
                landed(p, z - d, c)
                line(p, z - d, False, True)

    def multiply(r, d):
        def go(n, carry):
            side, cc = n % 2, n // 2
            zz = z + d * (1 - 2 * side)
            ok = (zz >= 0) & (zz < NZ)
            if d == 0:
                ok = ok & (side == 0)

            @pl.when(ok)
            def _():
                @pl.when(cc != c)
                def _():
                    for h in range(HEAD_CUTS):
                        landed(r * HEAD_CUTS + h, zz, cc)

                k = (zz // 2 + z // 2) % 2
                for o in range(2):
                    total = acc[r, k, o]
                    for h in range(HEAD_CUTS):
                        start = (cc * HEAD_CUTS + h) * part
                        rows = pl.ds(pl.multiple_of(start, part), part)
                        total += jnp.dot(
                            buf[r * HEAD_CUTS + h, zz * 2 + cc],
                            proj_ref[o, zz % 2, rows, :],
                            preferred_element_type=F32,
                        )
                    acc[r, k, o] = total

            return carry

        lax.fori_loop(0, 4, go, 0)

    for slot in range(5):
        fetch(*loads[slot], slot).wait()
    visible = len_ref[me // KVH]

    def attention(r, h):
        keys = slice(0, (r + 1) * tall)

        def head(n, carry):
            src = pl.ds(pl.multiple_of(h * part + n * HD, HD), HD)
            dst = pl.ds(pl.multiple_of(n * HD, HD), HD)
            buf[r * HEAD_CUTS + h, z * 2 + c, :, dst] = attend(
                q_ref[r * tall : (r + 1) * tall, src], ck_ref[...], cv_ref[...],
                nk_ref[keys], nv_ref[keys], visible, r * tall,
            )
            return carry

        lax.fori_loop(0, part // HD, head, 0)

    ids_got[me] = jnp.concatenate([ids_ref[0], ids_ref[1]], axis=1)
    attention(0, 0)
    greeted()
    line(0, z, True, True)
    for slot in range(9, 13):
        fetch(*loads[slot], slot).wait()
    for q in range(2):
        for n in range(2):
            swap(q, n).start()
    others(me, lambda dev: ids_copy(me, dev).start())
    for r in range(ROW_CUTS):
        for h in range(HEAD_CUTS):
            if r or h:
                attention(r, h)
                line(r * HEAD_CUTS + h, z, True, True)
    fetch(*loads[7], 7).wait()

    def restage(n, carry):
        start = n * width
        raw = hid_raw[:, :, pl.ds(pl.multiple_of(start, width), width)].astype(F32)
        rows = raw.reshape(mine, width).astype(BF16)
        cols = pl.ds(
            pl.multiple_of(half_at + n % (NDEV // 2) * width, width), width
        )
        moved = jnp.dot(order(), rows, preferred_element_type=F32).astype(BF16)
        gu[spare + n // (NDEV // 2), 0:mine, cols] = moved

        @pl.when(n == me)
        def _():
            hid_got[me] = moved

        return carry

    lax.fori_loop(0, NDEV, restage, 0)
    others(me, lambda dev: hid_copy(dev).start())
    acc[...] = jnp.zeros_like(acc)
    acts[...] = jnp.zeros_like(acts)
    ss_ref[...] = jnp.zeros_like(ss_ref)
    lg_ref[...] = jnp.zeros_like(lg_ref)

    def ranks(ids, block):
        lanes = ids.shape[1]
        rows = lax.broadcasted_iota(jnp.int32, (EXPERTS, lanes), 0)
        first = (ids[0:1] == rows).astype(F32)
        second = (ids[1:2] == rows).astype(F32)
        one = lax.broadcasted_iota(jnp.int32, (lanes, lanes), 0)
        two = lax.broadcasted_iota(jnp.int32, (lanes, lanes), 1)
        same = (one // block) == (two // block)
        tri = ((one < two) & same).astype(F32)
        before0 = jnp.dot(first, tri, preferred_element_type=F32)
        before1 = jnp.dot(second, tri, preferred_element_type=F32) + jnp.dot(
            first, same.astype(F32), preferred_element_type=F32
        )
        return (
            jnp.sum(before0 * first, axis=0, keepdims=True),
            jnp.sum(before1 * second, axis=0, keepdims=True),
        )

    def own_places():
        ids = ids_got[me]
        spots = lax.broadcasted_iota(jnp.int32, (SLOTS, mine), 0).astype(F32)
        total = jnp.zeros((SLOTS, mine), F32)
        for k, rank in enumerate(ranks(ids, mine)):
            expert = ids[k : k + 1].astype(F32)
            where = jnp.where(rank < MAIN - 0.5, expert * MAIN + rank, EXPERTS * MAIN + expert)
            total += (spots == where).astype(F32)
        place_ref[...] = total.T.astype(BF16)

    def codes():
        others(me, lambda dev: ids_copy(dev, dev).wait_recv())
        for q in range(NDEV // 2):
            ids = jnp.concatenate([ids_got[2 * q], ids_got[2 * q + 1]], axis=1)
            r, at = 2 * q // BLOCKS, (2 * q % BLOCKS) * mine
            lane = lax.broadcasted_iota(jnp.int32, (1, 2 * mine), 1)
            block = ((at + lane) // mine).astype(F32)
            cols = slice(at, at + 2 * mine)
            for k, rank in enumerate(ranks(ids, mine)):
                name = ids[k : k + 1].astype(F32)
                spot = jnp.where(rank < MAIN - 0.5, block * MAIN + rank, BLOCKS * MAIN + block)
                code_ref[r, k : k + 1, cols] = name * PART_SLOTS + spot
                name_ref[r, k : k + 1, cols] = name

    def spots_of(e):
        rows = lax.broadcasted_iota(jnp.int32, (PART_SLOTS, span), 0)
        return (rows + e * PART_SLOTS).astype(F32)

    def selects(r):
        def go(e, carry):
            spots = spots_of(e)
            hit = (spots == code_ref[r, 0:1, :]) | (spots == code_ref[r, 1:2, :])
            sel_ref[r, e] = hit.astype(F32).astype(BF16)
            return carry

        lax.fori_loop(0, EXPERTS, go, 0)

    def infos():
        for r in range(ROW_CUTS):
            spots = spots_of(me)
            hit0 = (spots == code_ref[r, 0:1, :]).astype(F32)
            hit1 = (spots == code_ref[r, 1:2, :]).astype(F32)
            chosen = jnp.sum(hit0, axis=1, keepdims=True)
            other = jnp.sum(
                hit0 * name_ref[r, 1:2, :] + hit1 * name_ref[r, 0:1, :], axis=1, keepdims=True
            )
            rows = slice(r * PART_SLOTS, (r + 1) * PART_SLOTS)
            info_ref[0, rows, :] = jnp.broadcast_to(chosen, (PART_SLOTS, info_ref.shape[2]))
            info_ref[1, rows, :] = jnp.broadcast_to(other, (PART_SLOTS, info_ref.shape[2]))

    def go_copy(r, src, dev):
        return remote(
            out_go.at[r, dev], out_got.at[r, src], go_send.at[r, dev], go_recv.at[r, src], dev
        )

    def residual(r):
        for b in range(BLOCKS):
            for s in range(2):
                rows = slice(b * piece, (b + 1) * piece)
                at = b * mine + s * piece
                k = (s + z // 2) % 2
                value = acc[r, k, 0, rows, :] + part_got[r, k, rows, :].astype(F32)
                value += hid_got[r * BLOCKS + b, s * piece : (s + 1) * piece, :].astype(F32)
                resid[at : at + piece, :] = value.astype(BF16)

    def select(r, dev):
        return jnp.dot(sel_ref[r, dev], resid[...], preferred_element_type=F32).astype(BF16)

    def first_send(i, carry):
        dev = (me + 7 * i) % NDEV
        out_go[0, dev] = select(0, dev)
        go_copy(0, me, dev).start()
        return carry

    def last_sends(s, step):
        for n in range(2):
            dev = chip_at(s) * 2 + n
            if isinstance(s, int) and s == 0:
                @pl.when(dev != me)
                def _():
                    step(go_copy(1, me, dev))
            else:
                step(go_copy(1, me, dev))

    def last_select(s):
        for n in range(2):
            dev = chip_at(s) * 2 + n
            out_go[1, dev] = select(1, dev)

    arrive(0, 1)
    own_places()
    arrive(1, 1)
    codes()
    arrive(0, 2)
    selects(0)
    infos()
    arrive(1, 2)
    for q in range(2):
        fetch(*loads[5 + q], 5 + q).wait()
        for n in range(2):
            swap(q, n).wait()
    others(me, lambda dev: hid_copy(dev).wait_send())
    for u in range(spare, GU_SLOTS):
        gate_up(u // 2, u % 2).start()
    multiply(0, 0)
    multiply(0, 1)
    share(0, 0)
    selects(1)
    multiply(0, 2)
    arrive(0, 3)
    multiply(0, 3)
    share(0, 1)
    multiply(1, 0)
    multiply(1, 1)
    share(1, 0)
    others(me, hid_landed)
    for k in range(2):
        share_copy(0, k).wait_recv()
    residual(0)
    lax.fori_loop(1, NDEV, first_send, 0)
    out_got[0, me] = select(0, me)
    multiply(1, 2)
    arrive(1, 3)
    multiply(1, 3)
    share(1, 1)
    for k in range(2):
        share_copy(1, k).wait_recv()
    residual(1)
    for s in (4, 5, 1, 2, 3, 0, 6, 7):
        last_select(s)
        if s < 6:
            last_sends(s, lambda copy: copy.start())
    out_got[1, me] = out_go[1, me]
    fetch(*loads[8], 8).wait()

    def gather(ref, dev, at):
        for r in range(ROW_CUTS):
            rows = slice(r * PART_SLOTS, (r + 1) * PART_SLOTS)
            ref[rows, at : at + width] = out_got[r, dev].astype(F32)

    steps = model // wide

    def take(s):
        chip = chip_at(s)
        for n in range(2):
            dev = chip * 2 + n

            @pl.when(dev != me)
            def _():
                for r in range(ROW_CUTS):
                    go_copy(r, dev, dev).wait_recv()

            gather(raw_ref, dev, n * width)
        raw = raw_ref[...]
        cols = pl.ds(pl.multiple_of(chip * wide, wide), wide)
        xg_ref[...] = (raw * gain_ref[:, cols]).astype(BF16)
        ss_ref[...] += jnp.broadcast_to(jnp.sum(raw * raw, axis=1, keepdims=True), ss_ref.shape)
        lg_ref[...] += lax.dot_general(
            xg_ref[...], router_ref[:, cols], (((1,), (1,)), ((), ())), preferred_element_type=F32
        )
        for n in range(2):
            gate_up(s, n).wait()

    def products(s):
        def one(n, carry):
            acts[n] += jnp.dot(
                xg_ref[...], gu[(2 * s + n) % GU_SLOTS], preferred_element_type=F32
            )
            return carry

        lax.fori_loop(0, 2, one, 0)

    def expert_step(s, carry):
        @pl.when((s == 2) | (s == 3))
        def _():
            last_sends(s + 2, lambda copy: copy.wait_send())
            last_sends(s + 4, lambda copy: copy.start())

        take(s)
        products(s)

        for n in range(2):
            at = 2 * s + n + GU_SLOTS

            @pl.when(at < 2 * steps)
            def _():
                gate_up(s + (n + GU_SLOTS) // 2, (n + GU_SLOTS) % 2).start()

        return carry

    lax.fori_loop(0, steps - 1, expert_step, 0)
    take(steps - 1)
    products(steps - 1)
    scale = lax.rsqrt(ss_ref[:, 0:1] / model + 1e-05)
    names = lax.broadcasted_iota(jnp.int32, lg_ref.shape, 1).astype(F32)
    mine_at = (names == me.astype(F32)).astype(F32)
    other_at = (names == info_ref[1, :, 0:1]).astype(F32)
    gap = jnp.sum(lg_ref[...] * (mine_at - other_at), axis=1, keepdims=True) * scale
    info_ref[1] = jnp.broadcast_to(jax.nn.sigmoid(gap), info_ref.shape[1:])

    def last_step(t, carry):
        cols = pl.ds(pl.multiple_of(t * TILE, TILE), TILE)
        gate, up = acts[0, :, cols] * scale, acts[1, :, cols] * scale
        inner[:, cols] = (gate / (1.0 + jnp.exp(-gate)) * up).astype(BF16)
        return carry

    lax.fori_loop(0, TILES, last_step, 0)
    chunks = back_go.shape[0]
    fold = BACK // MAIN

    def pack(store, values):
        for r in range(ROW_CUTS):
            at = r * PART_SLOTS
            cut = at + BLOCKS * MAIN
            blocks = slice(r * BLOCKS, (r + 1) * BLOCKS)
            for q in range(MAIN):
                fold_back[blocks, q, :] = values[cut : cut + BLOCKS, q * fold : (q + 1) * fold]
            store[blocks, :, :BACK] = values[at:cut].astype(BF16).reshape(BLOCKS, MAIN, BACK)
        store[:, :, BACK:] = fold_back[...].astype(BF16)

    def unpack(store):
        cut = EXPERTS * MAIN
        terms[:cut] = store[:, :, :BACK].reshape(cut, BACK)
        fold_back[...] = store[:, :, BACK:].astype(F32)
        for q in range(MAIN):
            terms[cut:, q * fold : (q + 1) * fold] = fold_back[:, q, :].astype(BF16)

    def back_copy(n, src, dev):
        return remote(
            back_go.at[n, dev], back_got.at[n, src], back_send.at[n, dev], back_recv.at[n, src], dev
        )

    def down_step(n, carry):
        for i in range(BACK // width):
            gather(back_raw, n * (BACK // width) + i, i * width)
        for i in range(DN_SLOTS):
            m = n * DN_SLOTS + i
            down(m).wait()
            cols = slice(i * DN_COLS, (i + 1) * DN_COLS)
            term = jnp.dot(inner[...], dn[i], preferred_element_type=F32)
            back_raw[:, cols] = (
                info_ref[1, :, 0:1] * term + info_ref[0, :, 0:1] * back_raw[:, cols]
            )

            @pl.when(n + 1 < chunks)
            def _():
                down(m + DN_SLOTS).start()

        pack(back_go.at[n], back_raw)
        others(me, lambda dev: back_copy(n, me, dev).start())
        back_got[n, me] = back_go[n, me]
        return carry

    lax.fori_loop(0, chunks, down_step, 0)

    def combine(n, carry):
        others(me, lambda dev: back_copy(n, dev, dev).wait_recv())
        unpack(back_got.at[n])
        cols = pl.ds(pl.multiple_of(n * BACK, BACK), BACK)
        out_ref[:, cols] = jnp.dot(
            place_ref[...], terms[...], preferred_element_type=F32
        ).astype(BF16)
        return carry

    lax.fori_loop(0, chunks, combine, 0)

    def finish(dev):
        ids_copy(me, dev).wait_send()
        go_copy(0, me, dev).wait_send()

        def sent(n, carry):
            back_copy(n, me, dev).wait_send()
            return carry

        lax.fori_loop(0, chunks, sent, 0)

    others(me, finish)
    for s in (0, 1, 2, 3, 6, 7):
        last_sends(s, lambda copy: copy.wait_send())
    for r in range(ROW_CUTS):
        for k in range(2):
            share_copy(r, k).wait_send()
    for p in range(PIECES):
        for zz in range(NZ):
            @pl.when((z > 0) & (zz >= z))
            def _():
                to_left(p, zz).wait_send()

            @pl.when((z < NZ - 1) & (zz <= z))
            def _():
                to_right(p, zz).wait_send()

            to_core(p, zz).wait_send()


def layer(cache_len, q, ck, cv, nk, nv, out_proj, hidden, gain, router, ids, gate_proj, up_proj, down_proj):
    rows, width = q.shape
    seqs = NDEV // KVH
    cols = out_proj.shape[1]
    mine, model = hidden.shape[0] * hidden.shape[1], hidden.shape[2]
    ffw = gate_proj.shape[1]
    chunks = model // BACK
    tall = rows // ROW_CUTS
    span = mine * BLOCKS
    dma = pltpu.SemaphoreType.DMA
    inside = pl.BlockSpec(memory_space=pltpu.VMEM)
    outside = pl.BlockSpec(memory_space=pl.ANY)
    go = (ROW_CUTS, NDEV, PART_SLOTS, cols)
    back = (chunks, NDEV, MAIN, BACK + BACK // MAIN)
    return pl.pallas_call(
        layer_kernel,
        out_shape=jax.ShapeDtypeStruct((mine, model), BF16),
        in_specs=[pl.BlockSpec(memory_space=pltpu.SMEM)]
        + [outside] * 7
        + [inside, outside, inside]
        + [outside] * 3,
        out_specs=inside,
        scratch_shapes=[
            pltpu.VMEM(q.shape, BF16),
            pltpu.VMEM(ck.shape, BF16),
            pltpu.VMEM(cv.shape, BF16),
            pltpu.VMEM(nk.shape, BF16),
            pltpu.VMEM(nv.shape, BF16),
            pltpu.VMEM((PIECES, 2 * NZ, tall, width // HEAD_CUTS), BF16),
            pltpu.VMEM((ROW_CUTS, seqs, 2, tall, cols), F32),
            pltpu.VMEM((ROW_CUTS, seqs, tall, cols), BF16),
            pltpu.VMEM((ROW_CUTS, seqs, tall, cols), BF16),
            pltpu.VMEM(hidden.shape, BF16),
            pltpu.VMEM((NDEV, mine, cols), BF16),
            pltpu.VMEM((NDEV, TOPK, mine), jnp.int32),
            pltpu.VMEM((2, 2, out_proj.shape[0] // 4, cols), BF16),
            pltpu.VMEM(router.shape, BF16),
            pltpu.VMEM((span, cols), BF16),
            pltpu.VMEM((ROW_CUTS, TOPK, span), F32),
            pltpu.VMEM((ROW_CUTS, TOPK, span), F32),
            pltpu.VMEM((ROW_CUTS, EXPERTS, PART_SLOTS, span), BF16),
            pltpu.VMEM((2, SLOTS, 128), F32),
            pltpu.VMEM((mine, SLOTS), BF16),
            pltpu.VMEM(go, BF16),
            pltpu.VMEM(go, BF16),
            pltpu.VMEM((SLOTS, 2 * cols), F32),
            pltpu.VMEM((SLOTS, 2 * cols), BF16),
            pltpu.VMEM((SLOTS, 128), F32),
            pltpu.VMEM((SLOTS, EXPERTS), F32),
            pltpu.VMEM((2, SLOTS, ffw), F32),
            pltpu.VMEM((SLOTS, ffw), BF16),
            pltpu.VMEM(back, BF16),
            pltpu.VMEM(back, BF16),
            pltpu.VMEM((NDEV, MAIN, BACK // MAIN), F32),
            pltpu.VMEM((SLOTS, BACK), F32),
            pltpu.VMEM((SLOTS, BACK), BF16),
            pltpu.VMEM((GU_SLOTS, 2 * cols, ffw), BF16),
            pltpu.VMEM((DN_SLOTS, ffw, DN_COLS), BF16),
            dma((13,)), dma((GU_SLOTS,)), dma((DN_SLOTS,)), dma((PIECES, 2 * NZ)),
            dma((PIECES, NZ)), dma((PIECES, NZ)), dma((PIECES, NZ)), dma((2, 2)), dma((2, 2)),
            dma((ROW_CUTS, seqs)), dma((ROW_CUTS, seqs)),
            dma((NDEV,)), dma((NDEV,)), dma((NDEV,)), dma((NDEV,)),
            dma((ROW_CUTS, NDEV)), dma((ROW_CUTS, NDEV)),
            dma((chunks, NDEV)), dma((chunks, NDEV)),
        ],
        compiler_params=pltpu.CompilerParams(
            collective_id=0, has_side_effects=True, vmem_limit_bytes=63 << 20
        ),
    )(cache_len, q, ck, cv, nk, nv, out_proj, hidden, gain, router, ids, gate_proj, up_proj, down_proj)


def body(
    hidden_in, queries, cache_keys, cache_values, new_keys, new_values, cache_len,
    out_proj, norm_gain, router, expert_ids, gate_proj, up_proj, down_proj,
):
    piece, seqs, model = hidden_in.shape
    out = layer(
        cache_len, queries[0], cache_keys[0], cache_values[0], new_keys[0], new_values[0],
        out_proj, hidden_in, norm_gain.reshape(1, model), router.T, expert_ids.transpose(1, 2, 0),
        gate_proj, up_proj, down_proj,
    )
    return out.reshape(seqs, piece, model).transpose(1, 0, 2)


def solution(mesh):
    placed = (
        P("ea", "rep", None),
        P(("rep", "ea"), None, None),
        P(("rep", "ea"), None, None),
        P(("rep", "ea"), None, None),
        P(("rep", "ea"), None, None),
        P(("rep", "ea"), None, None),
        P("rep"),
        P(None, "ea"),
        P(),
        P(),
        P("ea", "rep", None),
        P(None, "ea"),
        P(None, "ea"),
        P("ea", None),
    )
    plan = body if mesh.shape["ea"] == NDEV else wide_body
    return jax.shard_map(
        plan, mesh=mesh, in_specs=placed, out_specs=P("ea", "rep", None), check_vma=False
    )
```

```python
import functools
import math

import jax
import jax.numpy as jnp
from jax import lax
from jax.experimental import pallas as pl
from jax.experimental.pallas import tpu as pltpu
from jax.sharding import PartitionSpec as P

HQ = 32
KVH = 8
HD = 128
EXPERTS = 16
TOPK = 2
CAP = 9


def expert_terms(received, gate_proj, up_proj, down_proj):
    src_count, slot_count, model_width = received.shape
    flat_rows = received.reshape(src_count * slot_count, model_width)
    gate_val = jnp.dot(flat_rows, gate_proj, preferred_element_type=jnp.float32)
    up_val = jnp.dot(flat_rows, up_proj, preferred_element_type=jnp.float32)
    inner_act = (jax.nn.silu(gate_val) * up_val).astype(jnp.bfloat16)
    shard_term = jnp.dot(inner_act, down_proj, preferred_element_type=jnp.float32).astype(
        jnp.bfloat16
    )
    return shard_term.reshape(src_count, slot_count, model_width)


def expert_half(received, gate_proj, up_proj, down_proj):
    shard_term = expert_terms(received, gate_proj, up_proj, down_proj)
    return lax.all_to_all(shard_term, "ea", split_axis=0, concat_axis=0, tiled=True)


def route_rows(normed, route_ids, first_gate, gate_proj, up_proj, down_proj):
    row_count, model_width = normed.shape
    dev_count = lax.axis_size("ea")
    shard_count = dev_count // EXPERTS
    flat_ids = route_ids.reshape(-1)
    pair_count = flat_ids.shape[0]
    expert_cols = jnp.arange(EXPERTS, dtype=jnp.int32)
    one_hot = (flat_ids[:, None] == expert_cols[None, :]).astype(jnp.float32)
    pair_order = jnp.arange(pair_count, dtype=jnp.int32)
    earlier = (pair_order[:, None] > pair_order[None, :]).astype(jnp.float32)
    before = jnp.dot(earlier, one_hot, precision=lax.Precision.HIGHEST)
    slot_pos = jnp.sum(before * one_hot, axis=1).astype(jnp.int32)
    target = (flat_ids * CAP + slot_pos).reshape(row_count, TOPK)
    slot_ids = jnp.arange(EXPERTS * CAP, dtype=jnp.int32)
    select = (
        (target[None, :, 0] == slot_ids[:, None]) | (target[None, :, 1] == slot_ids[:, None])
    ).astype(jnp.bfloat16)
    packed = jnp.dot(select, normed, preferred_element_type=jnp.float32).astype(jnp.bfloat16)
    packed = jnp.broadcast_to(
        packed.reshape(EXPERTS, 1, CAP, model_width), (EXPERTS, shard_count, CAP, model_width)
    )
    packed = packed.reshape(dev_count, CAP, model_width)
    first_slots = (CAP + 1) // 2
    bounds = [(0, first_slots), (first_slots, CAP)]
    pieces = []
    for lower, upper in bounds:
        part_block = packed[:, lower:upper]
        pieces.append(
            (lambda received: expert_half(received, gate_proj, up_proj, down_proj))(
                lax.all_to_all(part_block, "ea", split_axis=0, concat_axis=0, tiled=True)
            )
        )
    returned = jnp.concatenate(pieces, axis=1)
    expert_out = jnp.sum(
        returned.reshape(EXPERTS, shard_count, CAP, model_width).astype(jnp.float32), axis=1
    )
    expert_out = expert_out.reshape(EXPERTS * CAP, model_width)
    picked = jnp.take(expert_out, target, axis=0)
    return first_gate * picked[:, 0] + (1.0 - first_gate) * picked[:, 1]


def wide_body(
    hidden_in,
    queries,
    cache_keys,
    cache_values,
    new_keys,
    new_values,
    cache_len,
    out_proj,
    norm_gain,
    router,
    expert_ids,
    gate_proj,
    up_proj,
    down_proj,
):
    dev_count = lax.axis_size("ea")
    dev_index = lax.axis_index("ea")
    new_rows = queries.shape[1]
    group_q = HQ // KVH
    seq_count = dev_count // KVH
    piece_rows = new_rows // dev_count
    cache_rows = cache_keys.shape[1]
    col_width = out_proj.shape[1]
    model_width = hidden_in.shape[2]
    score_scale = 1.0 / math.sqrt(HD)
    visible = lax.dynamic_index_in_dim(cache_len, dev_index // KVH, keepdims=False)
    position = (
        jnp.arange(new_rows, dtype=jnp.int32).reshape(dev_count, piece_rows).T.reshape(new_rows)
    )
    query_rows = (
        queries[0]
        .reshape(dev_count, piece_rows, group_q, HD)
        .transpose(1, 0, 2, 3)
        .reshape(new_rows, group_q, HD)
    )
    all_keys = jnp.concatenate([cache_keys[0], new_keys[0]], axis=0)
    all_values = jnp.concatenate([cache_values[0], new_values[0]], axis=0)
    key_pos = jnp.arange(cache_rows + new_rows, dtype=jnp.int32)
    allowed = jnp.where(
        key_pos[None, :] < cache_rows,
        key_pos[None, :] < visible,
        key_pos[None, :] - cache_rows <= position[:, None],
    )
    scores = (
        jnp.einsum("qhd,kd->hqk", query_rows, all_keys, preferred_element_type=jnp.float32)
        * score_scale
    )
    scores = jnp.where(allowed[None], scores, jnp.float32(-1e30))
    top_score = jnp.max(scores, axis=2, keepdims=True)
    exp_scores = jnp.exp(scores - top_score)
    attn_probs = (exp_scores / jnp.sum(exp_scores, axis=2, keepdims=True)).astype(jnp.bfloat16)
    attended = jnp.einsum("hqk,kd->qhd", attn_probs, all_values, preferred_element_type=jnp.float32)
    attended = attended.astype(jnp.bfloat16).reshape(new_rows, group_q * HD)
    local_rows = out_proj.reshape(KVH, group_q * HD, col_width).transpose(1, 0, 2)
    outgoing = jnp.broadcast_to(local_rows[:, None], (group_q * HD, seq_count, KVH, col_width))
    outgoing = outgoing.reshape(group_q * HD, dev_count, col_width)
    group_proj = lax.all_to_all(outgoing, "ea", split_axis=1, concat_axis=1, tiled=True).reshape(
        group_q * HD, model_width
    )
    head_part = jnp.dot(attended, group_proj, preferred_element_type=jnp.float32).astype(
        jnp.bfloat16
    )
    arrived = lax.all_to_all(
        head_part.reshape(piece_rows, dev_count, model_width),
        "ea",
        split_axis=1,
        concat_axis=1,
        tiled=True,
    )
    head_sum = jnp.sum(
        arrived.reshape(piece_rows, seq_count, KVH, model_width).astype(jnp.float32), axis=2
    )
    residual = hidden_in.astype(jnp.float32) + head_sum
    flat_res = residual.reshape(piece_rows * seq_count, model_width)
    mean_sq = jnp.mean(flat_res * flat_res, axis=1, keepdims=True)
    normed = (flat_res * lax.rsqrt(mean_sq + 1e-05) * norm_gain[None, :]).astype(jnp.bfloat16)
    logits = jnp.dot(normed, router, preferred_element_type=jnp.float32)
    route_ids = expert_ids.reshape(piece_rows * seq_count, TOPK)
    chosen = jnp.take_along_axis(logits, route_ids, axis=1)
    first_gate = jax.nn.sigmoid(chosen[:, 0:1] - chosen[:, 1:2])
    expert_mix = route_rows(normed, route_ids, first_gate, gate_proj, up_proj, down_proj)
    result_rows = (flat_res + expert_mix).astype(jnp.bfloat16)
    return result_rows.reshape(piece_rows, seq_count, model_width)


NZ = 4
NDEV = 16
MAIN = 8
SLOTS = EXPERTS * CAP
F32 = jnp.float32
BF16 = jnp.bfloat16


def attend(q, ck, cv, nk, nv, visible, first_row):
    contract = (((1,), (1,)), ((), ()))
    rows, cached, fresh = q.shape[0], ck.shape[0], nk.shape[0]
    scale = 1.0 / math.sqrt(HD)
    old = lax.dot_general(q, ck, contract, preferred_element_type=F32) * scale
    new = lax.dot_general(q, nk, contract, preferred_element_type=F32) * scale
    old_pos = lax.broadcasted_iota(jnp.int32, (rows, cached), 1)
    row_pos = lax.broadcasted_iota(jnp.int32, (rows, fresh), 0) + first_row
    new_pos = lax.broadcasted_iota(jnp.int32, (rows, fresh), 1)
    old = jnp.where(old_pos < visible, old, -1e30)
    new = jnp.where(new_pos <= row_pos, new, -1e30)
    top = jnp.maximum(
        jnp.max(old, axis=1, keepdims=True), jnp.max(new, axis=1, keepdims=True)
    )
    old = jnp.exp(old - top)
    new = jnp.exp(new - top)
    total = jnp.sum(old, axis=1, keepdims=True) + jnp.sum(new, axis=1, keepdims=True)
    mixed = jnp.dot(old.astype(BF16), cv, preferred_element_type=F32)
    mixed += jnp.dot(new.astype(BF16), nv, preferred_element_type=F32)
    return (mixed / total).astype(BF16)


def remote(src, dst, send, recv, dev):
    return pltpu.make_async_remote_copy(
        src_ref=src,
        dst_ref=dst,
        send_sem=send,
        recv_sem=recv,
        device_id={"ea": dev},
        device_id_type=pl.DeviceIdType.MESH,
    )


def greet(me):
    barrier = pltpu.get_barrier_semaphore()

    def hello(off, carry):
        pl.semaphore_signal(
            barrier,
            inc=1,
            device_id={"ea": lax.rem(me + off, NDEV)},
            device_id_type=pl.DeviceIdType.MESH,
        )
        return carry

    lax.fori_loop(1, NDEV, hello, 0)


def greeted():
    pl.semaphore_wait(pltpu.get_barrier_semaphore(), NDEV - 1)


def others(me, step):
    def go(off, carry):
        step(lax.rem(me + off, NDEV))
        return carry

    lax.fori_loop(1, NDEV, go, 0)


TILE = 640
TILES = 5
GU_SLOTS = 9
DN_SLOTS = 2
DN_COLS = 512
ROW_CUTS = 2
HEAD_CUTS = 2
PIECES = ROW_CUTS * HEAD_CUTS
BLOCKS = NDEV // ROW_CUTS
PART_SLOTS = BLOCKS * CAP
BACK = 1024


def layer_kernel(
    len_ref, q_hbm, ck_hbm, cv_hbm, nk_hbm, nv_hbm, proj_hbm, hid_hbm, gain_ref, router_hbm, ids_ref, gate_hbm, up_hbm, down_hbm,
    out_ref,
    q_ref, ck_ref, cv_ref, nk_ref, nv_ref,
    buf, acc, part_go, part_got, hid_raw, hid_got, ids_got, proj_ref, router_ref, resid, code_ref, name_ref, sel_ref, info_ref, place_ref,
    out_go, out_got, raw_ref, xg_ref, ss_ref, lg_ref, acts, inner, back_go, back_got, fold_back, back_raw, terms, gu, dn,
    in_sem, gu_sem, dn_sem,
    block_sem, left_sem, right_sem, core_sem, swap_send, swap_recv, part_send, part_recv,
    hid_send, hid_recv, ids_send, ids_recv, go_send, go_recv, back_send, back_recv,
):
    me = lax.axis_index("ea")
    model = gain_ref.shape[1]
    width = proj_ref.shape[3]
    quarter = proj_ref.shape[2]
    mine = hid_got.shape[1]
    piece = mine // 2
    tall, part = buf.shape[2], buf.shape[3]
    span = resid.shape[0]
    wide = gu.shape[1]
    z, y, c = me // 4, (me // 2) % 2, me % 2

    def index(zz, yy, cc):
        return (zz * 2 + yy) * 2 + cc

    def fetch(src, dst, slot):
        return pltpu.make_async_copy(src, dst, in_sem.at[slot])

    def proj_rows(q, yy):
        return proj_hbm.at[pl.ds(pl.multiple_of((q * 2 + yy) * quarter, quarter), quarter), :]

    def order():
        rows = lax.broadcasted_iota(jnp.int32, (mine, mine), 0)
        source = 2 * (rows % piece) + rows // piece
        lanes = lax.broadcasted_iota(jnp.int32, (mine, mine), 1)
        return (lanes == source).astype(F32).astype(BF16)

    loads = [
        (q_hbm, q_ref), (ck_hbm, ck_ref), (nk_hbm, nk_ref), (cv_hbm, cv_ref), (nv_hbm, nv_ref),
        (proj_rows(0, y), proj_ref.at[0, 0]), (proj_rows(1, y), proj_ref.at[0, 1]),
        (hid_hbm, hid_raw), (router_hbm, router_ref),
    ]
    spare = GU_SLOTS - 2
    half_at = model // 4
    for n in range(2):
        for q in range(2):
            loads.append((
                proj_rows(q, 1 - y).at[n * wide : (n + 1) * wide],
                gu.at[spare + n, :, q * width : (q + 1) * width],
            ))
    for slot in (0, 1, 2, 3, 4, 7, 9, 10, 11, 12, 5, 6, 8):
        fetch(*loads[slot], slot).start()
    greet(me)

    def chip_at(s):
        low = (z + s // 2) % 2
        high = (z // 2 + s // 4) % 2
        return (high * 2 + low) * 2 + (y + s) % 2

    def gate_up(s, n):
        rows = pl.ds(pl.multiple_of(chip_at(s) * wide, wide), wide)
        slot = (2 * s + n) % GU_SLOTS
        src = (gate_hbm, up_hbm)[n]
        return pltpu.make_async_copy(src.at[rows, :], gu.at[slot], gu_sem.at[slot])

    def down(n):
        cols = pl.ds(pl.multiple_of(n * DN_COLS, DN_COLS), DN_COLS)
        slot = n % DN_SLOTS
        return pltpu.make_async_copy(down_hbm.at[:, cols], dn.at[slot], dn_sem.at[slot])

    for u in range(spare):
        gate_up(u // 2, u % 2).start()
    for n in range(DN_SLOTS):
        down(n).start()

    def hid_copy(dev):
        start = half_at + dev % (NDEV // 2) * width
        cols = pl.ds(pl.multiple_of(start, width), width)
        return remote(
            gu.at[spare + dev // (NDEV // 2), 0:mine, cols], hid_got.at[me],
            hid_send.at[dev], hid_recv.at[me], dev,
        )

    def hid_landed(dev):
        remote(
            hid_got.at[me], hid_got.at[dev], hid_send.at[dev], hid_recv.at[dev], dev
        ).wait_recv()

    def ids_copy(src, dev):
        return remote(
            ids_got.at[src], ids_got.at[src], ids_send.at[dev], ids_recv.at[src], dev
        )

    def swap(q, n):
        return remote(
            gu.at[spare + n, :, q * width : (q + 1) * width],
            proj_ref.at[1, q, n * wide : (n + 1) * wide, :],
            swap_send.at[q, n], swap_recv.at[q, n], index(z, 1 - y, c),
        )

    def share_copy(r, k):
        return remote(
            part_go.at[r, k], part_got.at[r, k], part_send.at[r, k], part_recv.at[r, k],
            index(z, 1 - y, c),
        )

    def share(r, k):
        part_go[r, k] = acc[r, k, 1].astype(BF16)
        share_copy(r, k).start()

    def block_copy(p, zz, cc, sem, dev):
        blk = zz * 2 + cc
        return remote(buf.at[p, blk], buf.at[p, blk], sem, block_sem.at[p, blk], dev)

    def to_left(p, zz):
        return block_copy(p, zz, c, left_sem.at[p, zz], index(z - 1, y, c))

    def to_right(p, zz):
        return block_copy(p, zz, c, right_sem.at[p, zz], index(z + 1, y, c))

    def to_core(p, zz):
        return block_copy(p, zz, c, core_sem.at[p, zz], index(z, y, 1 - c))

    def landed(p, zz, cc):
        block_copy(p, zz, cc, core_sem.at[p, 0], index(z, y, 1 - c)).wait_recv()

    def line(p, zz, go_left, go_right):
        if go_left:
            @pl.when(z > 0)
            def _():
                to_left(p, zz).start()
        if go_right:
            @pl.when(z < NZ - 1)
            def _():
                to_right(p, zz).start()
        to_core(p, zz).start()

    def arrive(r, d):
        for h in range(HEAD_CUTS):
            p = r * HEAD_CUTS + h

            @pl.when(z + d < NZ)
            def _():
                landed(p, z + d, c)
                line(p, z + d, True, False)

            @pl.when(z - d >= 0)
            def _():
                landed(p, z - d, c)
                line(p, z - d, False, True)

    def multiply(r, d):
        def go(n, carry):
            side, cc = n % 2, n // 2
            zz = z + d * (1 - 2 * side)
            ok = (zz >= 0) & (zz < NZ)
            if d == 0:
                ok = ok & (side == 0)

            @pl.when(ok)
            def _():
                @pl.when(cc != c)
                def _():
                    for h in range(HEAD_CUTS):
                        landed(r * HEAD_CUTS + h, zz, cc)

                k = (zz // 2 + z // 2) % 2
                for o in range(2):
                    total = acc[r, k, o]
                    for h in range(HEAD_CUTS):
                        start = (cc * HEAD_CUTS + h) * part
                        rows = pl.ds(pl.multiple_of(start, part), part)
                        total += jnp.dot(
                            buf[r * HEAD_CUTS + h, zz * 2 + cc],
                            proj_ref[o, zz % 2, rows, :],
                            preferred_element_type=F32,
                        )
                    acc[r, k, o] = total

            return carry

        lax.fori_loop(0, 4, go, 0)

    for slot in range(5):
        fetch(*loads[slot], slot).wait()
    visible = len_ref[me // KVH]

    def attention(r, h):
        keys = slice(0, (r + 1) * tall)

        def head(n, carry):
            src = pl.ds(pl.multiple_of(h * part + n * HD, HD), HD)
            dst = pl.ds(pl.multiple_of(n * HD, HD), HD)
            buf[r * HEAD_CUTS + h, z * 2 + c, :, dst] = attend(
                q_ref[r * tall : (r + 1) * tall, src], ck_ref[...], cv_ref[...],
                nk_ref[keys], nv_ref[keys], visible, r * tall,
            )
            return carry

        lax.fori_loop(0, part // HD, head, 0)

    ids_got[me] = jnp.concatenate([ids_ref[0], ids_ref[1]], axis=1)
    attention(0, 0)
    greeted()
    line(0, z, True, True)
    for slot in range(9, 13):
        fetch(*loads[slot], slot).wait()
    for q in range(2):
        for n in range(2):
            swap(q, n).start()
    others(me, lambda dev: ids_copy(me, dev).start())
    for r in range(ROW_CUTS):
        for h in range(HEAD_CUTS):
            if r or h:
                attention(r, h)
                line(r * HEAD_CUTS + h, z, True, True)
    fetch(*loads[7], 7).wait()

    def restage(n, carry):
        start = n * width
        raw = hid_raw[:, :, pl.ds(pl.multiple_of(start, width), width)].astype(F32)
        rows = raw.reshape(mine, width).astype(BF16)
        cols = pl.ds(
            pl.multiple_of(half_at + n % (NDEV // 2) * width, width), width
        )
        moved = jnp.dot(order(), rows, preferred_element_type=F32).astype(BF16)
        gu[spare + n // (NDEV // 2), 0:mine, cols] = moved

        @pl.when(n == me)
        def _():
            hid_got[me] = moved

        return carry

    lax.fori_loop(0, NDEV, restage, 0)
    others(me, lambda dev: hid_copy(dev).start())
    acc[...] = jnp.zeros_like(acc)
    acts[...] = jnp.zeros_like(acts)
    ss_ref[...] = jnp.zeros_like(ss_ref)
    lg_ref[...] = jnp.zeros_like(lg_ref)

    def ranks(ids, block):
        lanes = ids.shape[1]
        rows = lax.broadcasted_iota(jnp.int32, (EXPERTS, lanes), 0)
        first = (ids[0:1] == rows).astype(F32)
        second = (ids[1:2] == rows).astype(F32)
        one = lax.broadcasted_iota(jnp.int32, (lanes, lanes), 0)
        two = lax.broadcasted_iota(jnp.int32, (lanes, lanes), 1)
        same = (one // block) == (two // block)
        tri = ((one < two) & same).astype(F32)
        before0 = jnp.dot(first, tri, preferred_element_type=F32)
        before1 = jnp.dot(second, tri, preferred_element_type=F32) + jnp.dot(
            first, same.astype(F32), preferred_element_type=F32
        )
        return (
            jnp.sum(before0 * first, axis=0, keepdims=True),
            jnp.sum(before1 * second, axis=0, keepdims=True),
        )

    def own_places():
        ids = ids_got[me]
        spots = lax.broadcasted_iota(jnp.int32, (SLOTS, mine), 0).astype(F32)
        total = jnp.zeros((SLOTS, mine), F32)
        for k, rank in enumerate(ranks(ids, mine)):
            expert = ids[k : k + 1].astype(F32)
            where = jnp.where(rank < MAIN - 0.5, expert * MAIN + rank, EXPERTS * MAIN + expert)
            total += (spots == where).astype(F32)
        place_ref[...] = total.T.astype(BF16)

    def codes():
        others(me, lambda dev: ids_copy(dev, dev).wait_recv())
        for q in range(NDEV // 2):
            ids = jnp.concatenate([ids_got[2 * q], ids_got[2 * q + 1]], axis=1)
            r, at = 2 * q // BLOCKS, (2 * q % BLOCKS) * mine
            lane = lax.broadcasted_iota(jnp.int32, (1, 2 * mine), 1)
            block = ((at + lane) // mine).astype(F32)
            cols = slice(at, at + 2 * mine)
            for k, rank in enumerate(ranks(ids, mine)):
                name = ids[k : k + 1].astype(F32)
                spot = jnp.where(rank < MAIN - 0.5, block * MAIN + rank, BLOCKS * MAIN + block)
                code_ref[r, k : k + 1, cols] = name * PART_SLOTS + spot
                name_ref[r, k : k + 1, cols] = name

    def spots_of(e):
        rows = lax.broadcasted_iota(jnp.int32, (PART_SLOTS, span), 0)
        return (rows + e * PART_SLOTS).astype(F32)

    def selects(r):
        def go(e, carry):
            spots = spots_of(e)
            hit = (spots == code_ref[r, 0:1, :]) | (spots == code_ref[r, 1:2, :])
            sel_ref[r, e] = hit.astype(F32).astype(BF16)
            return carry

        lax.fori_loop(0, EXPERTS, go, 0)

    def infos():
        for r in range(ROW_CUTS):
            spots = spots_of(me)
            hit0 = (spots == code_ref[r, 0:1, :]).astype(F32)
            hit1 = (spots == code_ref[r, 1:2, :]).astype(F32)
            chosen = jnp.sum(hit0, axis=1, keepdims=True)
            other = jnp.sum(
                hit0 * name_ref[r, 1:2, :] + hit1 * name_ref[r, 0:1, :], axis=1, keepdims=True
            )
            rows = slice(r * PART_SLOTS, (r + 1) * PART_SLOTS)
            info_ref[0, rows, :] = jnp.broadcast_to(chosen, (PART_SLOTS, info_ref.shape[2]))
            info_ref[1, rows, :] = jnp.broadcast_to(other, (PART_SLOTS, info_ref.shape[2]))

    def go_copy(r, src, dev):
        return remote(
            out_go.at[r, dev], out_got.at[r, src], go_send.at[r, dev], go_recv.at[r, src], dev
        )

    def residual(r):
        for b in range(BLOCKS):
            for s in range(2):
                rows = slice(b * piece, (b + 1) * piece)
                at = b * mine + s * piece
                k = (s + z // 2) % 2
                value = acc[r, k, 0, rows, :] + part_got[r, k, rows, :].astype(F32)
                value += hid_got[r * BLOCKS + b, s * piece : (s + 1) * piece, :].astype(F32)
                resid[at : at + piece, :] = value.astype(BF16)

    def select(r, dev):
        return jnp.dot(sel_ref[r, dev], resid[...], preferred_element_type=F32).astype(BF16)

    def first_send(i, carry):
        dev = (me + 7 * i) % NDEV
        out_go[0, dev] = select(0, dev)
        go_copy(0, me, dev).start()
        return carry

    def last_sends(s, step):
        for n in range(2):
            dev = chip_at(s) * 2 + n
            if isinstance(s, int) and s == 0:
                @pl.when(dev != me)
                def _():
                    step(go_copy(1, me, dev))
            else:
                step(go_copy(1, me, dev))

    def last_select(s):
        for n in range(2):
            dev = chip_at(s) * 2 + n
            out_go[1, dev] = select(1, dev)

    arrive(0, 1)
    own_places()
    arrive(1, 1)
    codes()
    arrive(0, 2)
    selects(0)
    infos()
    arrive(1, 2)
    for q in range(2):
        fetch(*loads[5 + q], 5 + q).wait()
        for n in range(2):
            swap(q, n).wait()
    others(me, lambda dev: hid_copy(dev).wait_send())
    for u in range(spare, GU_SLOTS):
        gate_up(u // 2, u % 2).start()
    multiply(0, 0)
    multiply(0, 1)
    share(0, 0)
    selects(1)
    multiply(0, 2)
    arrive(0, 3)
    multiply(0, 3)
    share(0, 1)
    others(me, hid_landed)
    for k in range(2):
        share_copy(0, k).wait_recv()
    residual(0)
    lax.fori_loop(1, NDEV, first_send, 0)
    out_got[0, me] = select(0, me)
    multiply(1, 0)
    multiply(1, 1)
    share(1, 0)
    multiply(1, 2)
    arrive(1, 3)
    multiply(1, 3)
    share(1, 1)
    for k in range(2):
        share_copy(1, k).wait_recv()
    residual(1)
    for s in (4, 5, 1, 2, 3, 0, 6, 7):
        last_select(s)
        if s < 6:
            last_sends(s, lambda copy: copy.start())
    out_got[1, me] = out_go[1, me]
    fetch(*loads[8], 8).wait()

    def gather(ref, dev, at):
        for r in range(ROW_CUTS):
            rows = slice(r * PART_SLOTS, (r + 1) * PART_SLOTS)
            ref[rows, at : at + width] = out_got[r, dev].astype(F32)

    steps = model // wide

    def take(s):
        chip = chip_at(s)
        for n in range(2):
            dev = chip * 2 + n

            @pl.when(dev != me)
            def _():
                for r in range(ROW_CUTS):
                    go_copy(r, dev, dev).wait_recv()

            gather(raw_ref, dev, n * width)
        raw = raw_ref[...]
        cols = pl.ds(pl.multiple_of(chip * wide, wide), wide)
        xg_ref[...] = (raw * gain_ref[:, cols]).astype(BF16)
        ss_ref[...] += jnp.broadcast_to(jnp.sum(raw * raw, axis=1, keepdims=True), ss_ref.shape)
        lg_ref[...] += lax.dot_general(
            xg_ref[...], router_ref[:, cols], (((1,), (1,)), ((), ())), preferred_element_type=F32
        )
        for n in range(2):
            gate_up(s, n).wait()

    def products(s):
        def one(n, carry):
            acts[n] += jnp.dot(
                xg_ref[...], gu[(2 * s + n) % GU_SLOTS], preferred_element_type=F32
            )
            return carry

        lax.fori_loop(0, 2, one, 0)

    def expert_step(s, carry):
        @pl.when((s == 2) | (s == 3))
        def _():
            last_sends(s + 2, lambda copy: copy.wait_send())
            last_sends(s + 4, lambda copy: copy.start())

        take(s)
        products(s)

        for n in range(2):
            at = 2 * s + n + GU_SLOTS

            @pl.when(at < 2 * steps)
            def _():
                gate_up(s + (n + GU_SLOTS) // 2, (n + GU_SLOTS) % 2).start()

        return carry

    lax.fori_loop(0, steps - 1, expert_step, 0)
    take(steps - 1)
    products(steps - 1)
    scale = lax.rsqrt(ss_ref[:, 0:1] / model + 1e-05)
    names = lax.broadcasted_iota(jnp.int32, lg_ref.shape, 1).astype(F32)
    mine_at = (names == me.astype(F32)).astype(F32)
    other_at = (names == info_ref[1, :, 0:1]).astype(F32)
    gap = jnp.sum(lg_ref[...] * (mine_at - other_at), axis=1, keepdims=True) * scale
    info_ref[1] = jnp.broadcast_to(jax.nn.sigmoid(gap), info_ref.shape[1:])

    def last_step(t, carry):
        cols = pl.ds(pl.multiple_of(t * TILE, TILE), TILE)
        gate, up = acts[0, :, cols] * scale, acts[1, :, cols] * scale
        inner[:, cols] = (gate / (1.0 + jnp.exp(-gate)) * up).astype(BF16)
        return carry

    lax.fori_loop(0, TILES, last_step, 0)
    chunks = back_go.shape[0]
    fold = BACK // MAIN

    def pack(store, values):
        for r in range(ROW_CUTS):
            at = r * PART_SLOTS
            cut = at + BLOCKS * MAIN
            blocks = slice(r * BLOCKS, (r + 1) * BLOCKS)
            for q in range(MAIN):
                fold_back[blocks, q, :] = values[cut : cut + BLOCKS, q * fold : (q + 1) * fold]
            store[blocks, :, :BACK] = values[at:cut].astype(BF16).reshape(BLOCKS, MAIN, BACK)
        store[:, :, BACK:] = fold_back[...].astype(BF16)

    def unpack(store):
        cut = EXPERTS * MAIN
        terms[:cut] = store[:, :, :BACK].reshape(cut, BACK)
        fold_back[...] = store[:, :, BACK:].astype(F32)
        for q in range(MAIN):
            terms[cut:, q * fold : (q + 1) * fold] = fold_back[:, q, :].astype(BF16)

    def back_copy(n, src, dev):
        return remote(
            back_go.at[n, dev], back_got.at[n, src], back_send.at[n, dev], back_recv.at[n, src], dev
        )

    def down_step(n, carry):
        for i in range(BACK // width):
            gather(back_raw, n * (BACK // width) + i, i * width)
        for i in range(DN_SLOTS):
            m = n * DN_SLOTS + i
            down(m).wait()
            cols = slice(i * DN_COLS, (i + 1) * DN_COLS)
            term = jnp.dot(inner[...], dn[i], preferred_element_type=F32)
            back_raw[:, cols] = (
                info_ref[1, :, 0:1] * term + info_ref[0, :, 0:1] * back_raw[:, cols]
            )

            @pl.when(n + 1 < chunks)
            def _():
                down(m + DN_SLOTS).start()

        pack(back_go.at[n], back_raw)
        others(me, lambda dev: back_copy(n, me, dev).start())
        back_got[n, me] = back_go[n, me]
        return carry

    lax.fori_loop(0, chunks, down_step, 0)

    def combine(n, carry):
        others(me, lambda dev: back_copy(n, dev, dev).wait_recv())
        unpack(back_got.at[n])
        cols = pl.ds(pl.multiple_of(n * BACK, BACK), BACK)
        out_ref[:, cols] = jnp.dot(
            place_ref[...], terms[...], preferred_element_type=F32
        ).astype(BF16)
        return carry

    lax.fori_loop(0, chunks, combine, 0)

    def finish(dev):
        ids_copy(me, dev).wait_send()
        go_copy(0, me, dev).wait_send()

        def sent(n, carry):
            back_copy(n, me, dev).wait_send()
            return carry

        lax.fori_loop(0, chunks, sent, 0)

    others(me, finish)
    for s in (0, 1, 2, 3, 6, 7):
        last_sends(s, lambda copy: copy.wait_send())
    for r in range(ROW_CUTS):
        for k in range(2):
            share_copy(r, k).wait_send()
    for p in range(PIECES):
        for zz in range(NZ):
            @pl.when((z > 0) & (zz >= z))
            def _():
                to_left(p, zz).wait_send()

            @pl.when((z < NZ - 1) & (zz <= z))
            def _():
                to_right(p, zz).wait_send()

            to_core(p, zz).wait_send()


def layer(cache_len, q, ck, cv, nk, nv, out_proj, hidden, gain, router, ids, gate_proj, up_proj, down_proj):
    rows, width = q.shape
    seqs = NDEV // KVH
    cols = out_proj.shape[1]
    mine, model = hidden.shape[0] * hidden.shape[1], hidden.shape[2]
    ffw = gate_proj.shape[1]
    chunks = model // BACK
    tall = rows // ROW_CUTS
    span = mine * BLOCKS
    dma = pltpu.SemaphoreType.DMA
    inside = pl.BlockSpec(memory_space=pltpu.VMEM)
    outside = pl.BlockSpec(memory_space=pl.ANY)
    go = (ROW_CUTS, NDEV, PART_SLOTS, cols)
    back = (chunks, NDEV, MAIN, BACK + BACK // MAIN)
    return pl.pallas_call(
        layer_kernel,
        out_shape=jax.ShapeDtypeStruct((mine, model), BF16),
        in_specs=[pl.BlockSpec(memory_space=pltpu.SMEM)]
        + [outside] * 7
        + [inside, outside, inside]
        + [outside] * 3,
        out_specs=inside,
        scratch_shapes=[
            pltpu.VMEM(q.shape, BF16),
            pltpu.VMEM(ck.shape, BF16),
            pltpu.VMEM(cv.shape, BF16),
            pltpu.VMEM(nk.shape, BF16),
            pltpu.VMEM(nv.shape, BF16),
            pltpu.VMEM((PIECES, 2 * NZ, tall, width // HEAD_CUTS), BF16),
            pltpu.VMEM((ROW_CUTS, seqs, 2, tall, cols), F32),
            pltpu.VMEM((ROW_CUTS, seqs, tall, cols), BF16),
            pltpu.VMEM((ROW_CUTS, seqs, tall, cols), BF16),
            pltpu.VMEM(hidden.shape, BF16),
            pltpu.VMEM((NDEV, mine, cols), BF16),
            pltpu.VMEM((NDEV, TOPK, mine), jnp.int32),
            pltpu.VMEM((2, 2, out_proj.shape[0] // 4, cols), BF16),
            pltpu.VMEM(router.shape, BF16),
            pltpu.VMEM((span, cols), BF16),
            pltpu.VMEM((ROW_CUTS, TOPK, span), F32),
            pltpu.VMEM((ROW_CUTS, TOPK, span), F32),
            pltpu.VMEM((ROW_CUTS, EXPERTS, PART_SLOTS, span), BF16),
            pltpu.VMEM((2, SLOTS, 128), F32),
            pltpu.VMEM((mine, SLOTS), BF16),
            pltpu.VMEM(go, BF16),
            pltpu.VMEM(go, BF16),
            pltpu.VMEM((SLOTS, 2 * cols), F32),
            pltpu.VMEM((SLOTS, 2 * cols), BF16),
            pltpu.VMEM((SLOTS, 128), F32),
            pltpu.VMEM((SLOTS, EXPERTS), F32),
            pltpu.VMEM((2, SLOTS, ffw), F32),
            pltpu.VMEM((SLOTS, ffw), BF16),
            pltpu.VMEM(back, BF16),
            pltpu.VMEM(back, BF16),
            pltpu.VMEM((NDEV, MAIN, BACK // MAIN), F32),
            pltpu.VMEM((SLOTS, BACK), F32),
            pltpu.VMEM((SLOTS, BACK), BF16),
            pltpu.VMEM((GU_SLOTS, 2 * cols, ffw), BF16),
            pltpu.VMEM((DN_SLOTS, ffw, DN_COLS), BF16),
            dma((13,)), dma((GU_SLOTS,)), dma((DN_SLOTS,)), dma((PIECES, 2 * NZ)),
            dma((PIECES, NZ)), dma((PIECES, NZ)), dma((PIECES, NZ)), dma((2, 2)), dma((2, 2)),
            dma((ROW_CUTS, seqs)), dma((ROW_CUTS, seqs)),
            dma((NDEV,)), dma((NDEV,)), dma((NDEV,)), dma((NDEV,)),
            dma((ROW_CUTS, NDEV)), dma((ROW_CUTS, NDEV)),
            dma((chunks, NDEV)), dma((chunks, NDEV)),
        ],
        compiler_params=pltpu.CompilerParams(
            collective_id=0, has_side_effects=True, vmem_limit_bytes=63 << 20
        ),
    )(cache_len, q, ck, cv, nk, nv, out_proj, hidden, gain, router, ids, gate_proj, up_proj, down_proj)


def body(
    hidden_in, queries, cache_keys, cache_values, new_keys, new_values, cache_len,
    out_proj, norm_gain, router, expert_ids, gate_proj, up_proj, down_proj,
):
    piece, seqs, model = hidden_in.shape
    out = layer(
        cache_len, queries[0], cache_keys[0], cache_values[0], new_keys[0], new_values[0],
        out_proj, hidden_in, norm_gain.reshape(1, model), router.T, expert_ids.transpose(1, 2, 0),
        gate_proj, up_proj, down_proj,
    )
    return out.reshape(seqs, piece, model).transpose(1, 0, 2)


def solution(mesh):
    placed = (
        P("ea", "rep", None),
        P(("rep", "ea"), None, None),
        P(("rep", "ea"), None, None),
        P(("rep", "ea"), None, None),
        P(("rep", "ea"), None, None),
        P(("rep", "ea"), None, None),
        P("rep"),
        P(None, "ea"),
        P(),
        P(),
        P("ea", "rep", None),
        P(None, "ea"),
        P(None, "ea"),
        P("ea", None),
    )
    plan = body if mesh.shape["ea"] == NDEV else wide_body
    return jax.shard_map(
        plan, mesh=mesh, in_specs=placed, out_specs=P("ea", "rep", None), check_vma=False
    )
```
